32 devices in a mesh: wide: 4 (over y, core), sixteen: 8 (over z, x).
Axes of the slice: x: 2, y: 2, z: 4, core: 2. Of those that a mesh axis runs over, the one named last changes fastest.
Arguments:
- observations: float32 [64, 256, 512], P(None, 'sixteen', 'wide'), may hold values from -60 to 60
- huber_scale: float32 [64], replicated, may hold values from 0.5 to 2
- observed: int32 [256, 512], P('sixteen', 'wide'), may hold values from 0 to 1, as said below
- jitter: float32 [2, 256, 512], P(None, 'sixteen', 'wide'), may hold values from -0.4 to 0.4
- owner_map: int32 [4, 64], P('wide'), may hold values from 0 to 7, as said below
- neighbours: int32 [4, 64, 6], P('wide'), may hold values from 0 to 63, as said below
Outputs:
- solution: float32 [4, 8, 64, 8, 512], P('wide', 'sixteen')
- residual: float32 [4, 8, 64, 8, 512], P('wide', 'sixteen')
The draws below stay inside these ranges and needn't reach their ends.
Inputs may be any that keep to these rules, and one draw needn't show every extreme that they name: At least one whole lattice row and at least one whole lattice column hold no observed point. `owner_map`: in each column group every device along sixteen holds 8 blocks (block g on device g // 8) and sends them to 8 different owners; every owner receives exactly 8 blocks, each from a different device. `neighbours`: block g of a column group lists g + d and g - d modulo 64 for each of half of 6 different offsets d between 1 and 4; all blocks of one group use the same offsets, so every list holds 6 different blocks and the relation is symmetric.
All inputs are finite; a program needn't handle non-finite values.
Results may differ from the reference program's by a relative error of at most 0.0003.
Values sent between devices are 32-bit elements; how exact they have to be, the bound alone decides.
A program may use at most 192 MiB of HBM per device.

```python
import math
import jax
import jax.numpy as jnp
from jax import lax

FIELDS = 64
BLOCK = 512
COL_DEV = 128
BLOCKS_DEV = 8
REACH = 4
NEIGHBOURS = 6
SWEEPS = 2
ITERS = 2
STRIP = 4
NSTRIPS = 64
NROW = 256
NCOL = 512
N_WIDE = 4
N_SIXTEEN = 8


def draw_observations(key, part):
    first_key, second_key, third_key, random_key_four = jax.random.split(jax.random.fold_in(key, 11), 4)
    lattice_dimensions = (FIELDS, NROW, NCOL)
    row_coefficients = jax.random.normal(first_key, (FIELDS, NROW, 1), jnp.float32)
    column_coefficients = jax.random.normal(second_key, (FIELDS, 1, NCOL), jnp.float32)
    gaussian_jitter = jax.random.normal(third_key, lattice_dimensions, jnp.float32)
    outlier_spikes = jnp.where(jax.random.uniform(random_key_four, lattice_dimensions, jnp.float32) < 0.05, 6.0, 0.0) * jnp.sign(gaussian_jitter + 0.001)
    observed_values = 1.5 * row_coefficients + 1.5 * column_coefficients + gaussian_jitter + outlier_spikes
    return jnp.clip(observed_values, -60.0, 60.0).astype(jnp.float32)


def draw_observed(key, part):
    first_key, second_key, third_key = jax.random.split(jax.random.fold_in(key, 53), 3)
    base = jax.random.randint(first_key, (NROW, NCOL), 0, 8) < 7
    empty_rows = jax.random.randint(second_key, (2,), 0, NROW)
    empty_cols = jax.random.randint(third_key, (2,), 0, NCOL)
    rows_hit = jnp.any(jnp.arange(NROW, dtype=jnp.int32)[:, None] == empty_rows[None, :], axis=1)
    cols_hit = jnp.any(jnp.arange(NCOL, dtype=jnp.int32)[:, None] == empty_cols[None, :], axis=1)
    cleared = rows_hit[:, None] | cols_hit[None, :]
    return jnp.where(cleared, 0, base.astype(jnp.int32)).astype(jnp.int32)


def draw_owner_map(key, part):

    def one_group(group_key):
        first_key, second_key, third_key = jax.random.split(group_key, 3)
        sources = jax.random.permutation(first_key, N_SIXTEEN)
        owners = jax.random.permutation(second_key, N_SIXTEEN)
        orders = jax.vmap(lambda order_key: jax.random.permutation(order_key, BLOCKS_DEV))(jax.random.split(third_key, N_SIXTEEN))
        return owners[(sources[:, None] + orders) % N_SIXTEEN].reshape(-1)
    group_keys = jax.random.split(jax.random.fold_in(key, 23), N_WIDE)
    return jax.vmap(one_group)(group_keys).astype(jnp.int32)


def draw_neighbours(key, part):
    total_strips = BLOCKS_DEV * N_SIXTEEN

    def one_group(group_key):
        offsets = jax.random.permutation(group_key, REACH)[:NEIGHBOURS // 2] + 1
        signed = jnp.stack([offsets, -offsets], axis=1).reshape(-1)
        numbers = jnp.arange(total_strips, dtype=jnp.int32)
        return (numbers[:, None] + signed[None, :]) % total_strips
    group_keys = jax.random.split(jax.random.fold_in(key, 37), N_WIDE)
    return jax.vmap(one_group)(group_keys).astype(jnp.int32)


def level_of(key, shape, cuts, least, top_value):
    def one(position, blocks):
        draws = jax.random.uniform(jax.random.fold_in(jax.random.fold_in(key, 6), position), (blocks,), jnp.float32, least / len(cuts), top_value / len(cuts))
        return jnp.repeat(jnp.exp(draws), shape[position] // blocks).reshape((-1,) + (1,) * (len(shape) - position - 1))

    level = one(*cuts[0])
    for cut in cuts[1:]:
        level = level * one(*cut)
    return level


def setup_inputs(seed: int = 0) -> dict:
    arg_keys = jax.random.split(jax.random.key(seed), 7)
    observations = draw_observations(jax.random.fold_in(arg_keys[6], 71), 0)
    huber_scale = jnp.clip(jnp.exp(jax.random.uniform(arg_keys[1], (FIELDS,), jnp.float32, math.log(0.5), math.log(2.0))), 0.5, 2.0)
    observed = draw_observed(jax.random.fold_in(arg_keys[6], 71), 0)
    jitter = jnp.clip(jax.random.uniform(arg_keys[3], (2, NROW, NCOL), jnp.float32, -0.4, 0.4) * level_of(arg_keys[3], (2, NROW, NCOL), ((1, 8), (2, 4)), -0.4, 0.0), -0.4, 0.4)
    owner_map = draw_owner_map(jax.random.fold_in(arg_keys[6], 71), 0)
    neighbours = draw_neighbours(jax.random.fold_in(arg_keys[6], 71), 0)
    return {"observations": observations, "huber_scale": huber_scale, "observed": observed, "jitter": jitter, "owner_map": owner_map, "neighbours": neighbours}


HUBER_EDGE = 1.345
NUGGET_TERM = 1.0
SILL_TERM = 0.02
ROOT_THREE = 1.7320508075688772
EXACT = lax.Precision.HIGHEST

def covariance(centre, others, strip_rows):
    spread = 2.0 * strip_rows
    cutoff = 6.0 * strip_rows
    row_gap = others[0][:, :, None] - centre[0][None, None, :]
    col_gap = others[1][:, :, None] - centre[1][None, None, :]
    distance = jnp.sqrt(row_gap * row_gap + col_gap * col_gap)
    scaled = ROOT_THREE * distance / spread
    fading = jnp.maximum(1.0 - distance / cutoff, 0.0)
    return SILL_TERM * (1.0 + scaled) * jnp.exp(-scaled) * fading ** 4 * (1.0 + 4.0 * distance / cutoff)

def owned_table(group_map, owners, per_owner):
    total_strips = group_map.shape[0]
    member = (group_map[None, :] == jnp.arange(owners, dtype=jnp.int32)[:, None]).astype(jnp.int32)
    ranked = jnp.cumsum(member, axis=1, dtype=jnp.int32) - 1
    slot_hit = (ranked[:, :, None] == jnp.arange(per_owner, dtype=jnp.int32)[None, None, :]).astype(jnp.int32) * member[:, :, None]
    numbers = jnp.arange(total_strips, dtype=jnp.int32)
    return lax.optimization_barrier(jnp.sum(slot_hit * numbers[None, :, None], axis=1, dtype=jnp.int32))

def apply_operator(direction, centres, neighbours):

    def one_block(flat_index):
        group = flat_index // NSTRIPS
        strip_number = flat_index % NSTRIPS
        group_values = direction[group]
        group_places = centres[group]
        listed = neighbours[group, strip_number]
        own = group_values[:, strip_number]
        near = jnp.take(group_values, listed, axis=1)
        centre = group_places[:, strip_number]
        others = jnp.concatenate([centre[:, None], jnp.take(group_places, listed, axis=1)], axis=1)
        kernel = covariance(centre, others, STRIP)
        stacked = jnp.concatenate([(NEIGHBOURS + 1.0) * own[:, None], near], axis=1)
        return NUGGET_TERM * own + jnp.einsum('fmb,mba->fa', stacked, kernel, precision=EXACT)
    result = lax.map(one_block, jnp.arange(N_WIDE * NSTRIPS, dtype=jnp.int32))
    return result.reshape(N_WIDE, NSTRIPS, FIELDS, BLOCK).transpose(0, 2, 1, 3)

def blocked(observed_values):
    depth = observed_values.shape[0]
    shaped = observed_values.reshape(depth, NSTRIPS, STRIP, N_WIDE, COL_DEV)
    return shaped.transpose(3, 0, 1, 2, 4).reshape(N_WIDE, depth, NSTRIPS, BLOCK)

def reference(observations, huber_scale, observed, jitter, owner_map, neighbours):
    weight = observed.astype(jnp.float32)
    row_count = jnp.maximum(lax.optimization_barrier(jnp.sum(weight, axis=1)), 1.0)
    col_count = jnp.maximum(lax.optimization_barrier(jnp.sum(weight, axis=0)), 1.0)
    spread_scale = huber_scale[:, None, None]
    row_effect = jnp.zeros((FIELDS, NROW), jnp.float32)
    col_effect = jnp.zeros((FIELDS, NCOL), jnp.float32)
    for sweep_number in range(SWEEPS):
        clipped = jnp.clip((observations - row_effect[:, :, None] - col_effect[:, None, :]) / spread_scale, -HUBER_EDGE, HUBER_EDGE)
        row_effect = row_effect + huber_scale[:, None] * lax.optimization_barrier(jnp.sum(weight[None] * clipped, axis=2)) / row_count[None, :]
        clipped = jnp.clip((observations - row_effect[:, :, None] - col_effect[:, None, :]) / spread_scale, -HUBER_EDGE, HUBER_EDGE)
        col_effect = col_effect + huber_scale[:, None] * lax.optimization_barrier(jnp.sum(weight[None] * clipped, axis=1)) / col_count[None, :]
    residual_field = weight[None] * (observations - row_effect[:, :, None] - col_effect[:, None, :])
    row_place = jnp.arange(NROW, dtype=jnp.int32).astype(jnp.float32)
    col_place = jnp.arange(NCOL, dtype=jnp.int32).astype(jnp.float32)
    location = jnp.stack([row_place[:, None] + jitter[0], col_place[None, :] + jitter[1]])
    right_side = blocked(residual_field)
    centres = blocked(location)
    solution_now = jnp.zeros_like(right_side)
    residual_now = right_side
    direction = right_side
    norm_now = lax.optimization_barrier(jnp.sum(residual_now * residual_now, axis=(0, 2, 3)))
    for number in range(ITERS):
        image = apply_operator(direction, centres, neighbours)
        alpha = norm_now / lax.optimization_barrier(jnp.sum(direction * image, axis=(0, 2, 3)))
        solution_now = solution_now + alpha[None, :, None, None] * direction
        residual_now = residual_now - alpha[None, :, None, None] * image
        if number + 1 < ITERS:
            norm_next = lax.optimization_barrier(jnp.sum(residual_now * residual_now, axis=(0, 2, 3)))
            direction = residual_now + (norm_next / norm_now)[None, :, None, None] * direction
            norm_now = norm_next
    table = jax.vmap(lambda group_map: owned_table(group_map, N_SIXTEEN, BLOCKS_DEV))(owner_map)

    def place(observed_values):

        def one_group(group_values, group_table):
            picked = jnp.take(group_values, group_table.reshape(-1), axis=1)
            return picked.reshape(FIELDS, N_SIXTEEN, BLOCKS_DEV, BLOCK).transpose(1, 0, 2, 3)
        return jax.vmap(one_group)(observed_values, table)
    return (place(solution_now), place(residual_now))
```

```python
import functools

import jax
import jax.numpy as jnp
from jax import lax
from jax.experimental import pallas as pl
from jax.experimental.pallas import tpu as pltpu
from jax.sharding import PartitionSpec as P

BLOCK = 512
BLOCKS_DEV = 8
REACH = 4
NEIGHBOURS = 6
SWEEPS = 2

HUBER_EDGE = 1.345
NUGGET_TERM = 1.0
SILL_TERM = 0.02
ROOT_THREE = 1.7320508075688772
LOG2E = 1.4426950408889634
GROUP = 16
MESH = pl.DeviceIdType.MESH
VMEM = pl.BlockSpec(memory_space=pltpu.VMEM)
SMEM = pl.BlockSpec(memory_space=pltpu.SMEM)


def owned_table(group_map, owners, per_owner):
    total_strips = group_map.shape[0]
    member = (group_map[None, :] == jnp.arange(owners, dtype=jnp.int32)[:, None]).astype(jnp.int32)
    ranked = jnp.cumsum(member, axis=1, dtype=jnp.int32) - 1
    slot_hit = (ranked[:, :, None] == jnp.arange(per_owner, dtype=jnp.int32)[None, None, :]).astype(
        jnp.int32
    ) * member[:, :, None]
    numbers = jnp.arange(total_strips, dtype=jnp.int32)
    return jnp.sum(slot_hit * numbers[None, :, None], axis=1, dtype=jnp.int32)


def greet(sizes):
    barrier = pltpu.get_barrier_semaphore()
    for axis, n in sizes:
        me = lax.axis_index(axis)

        def say(k, carry, axis=axis, n=n, me=me):
            pl.semaphore_signal(
                barrier, inc=1, device_id={axis: lax.rem(me + k, n)}, device_id_type=MESH
            )
            return carry

        lax.fori_loop(1, n, say, 0)
    pl.semaphore_wait(barrier, sum(n - 1 for _, n in sizes))


def all_sum(buffer, axis, n, send_sem, recv_sem):
    me = lax.axis_index(axis)

    def copy(k):
        return pltpu.make_async_remote_copy(
            src_ref=buffer.at[0],
            dst_ref=buffer.at[k],
            send_sem=send_sem.at[k],
            recv_sem=recv_sem.at[k],
            device_id={axis: lax.rem(me + k, n)},
            device_id_type=MESH,
        )

    copies = [copy(k) for k in range(1, n)]
    for c in copies:
        c.start()
    for c in copies:
        c.wait()
    total = None
    for owner in range(n):
        term = buffer[lax.rem(me - owner + n, n)]
        total = term if total is None else total + term
    return total


def swap(x):
    return pltpu.roll(x, x.shape[-1] // 2, x.ndim - 1)


def fold(x):
    return x + swap(x)


def halves(x, fields):
    return lax.broadcasted_iota(jnp.int32, x.shape, x.ndim - 1) < fields


def halo_copies(halo, rows, reach, n, send_sem, recv_sem, axis="sixteen"):
    me = lax.axis_index(axis)
    up, down = lax.rem(me + 1, n), lax.rem(me + n - 1, n)
    return [
        pltpu.make_async_remote_copy(
            src_ref=halo.at[pl.ds(rows, reach)],
            dst_ref=halo.at[pl.ds(0, reach)],
            send_sem=send_sem.at[0],
            recv_sem=recv_sem.at[0],
            device_id={axis: up},
            device_id_type=MESH,
        ),
        pltpu.make_async_remote_copy(
            src_ref=halo.at[pl.ds(reach, reach)],
            dst_ref=halo.at[pl.ds(reach + rows, reach)],
            send_sem=send_sem.at[1],
            recv_sem=recv_sem.at[1],
            device_id={axis: down},
            device_id_type=MESH,
        ),
    ]


def polish_kernel(
    nw, ns, fields, reach,
    obs, weight, scale, place, halo, place_halo, norm,
    row_eff, row_cnt, col_eff, col_cnt,
    row_buf0, row_buf1, col_buf0, col_buf1, norm_w, norm_s,
    sems_s, sems_r,
):
    rows, cols, lanes = obs.shape
    half = cols // 2
    place_rows = place.shape[0]
    place_reach = 2 * reach
    greet((("wide", nw), ("sixteen", ns)))
    place_halo[pl.ds(place_reach, place_rows)] = place[...]
    place_copies = halo_copies(
        place_halo, place_rows, place_reach, ns, sems_s.at[6], sems_r.at[6]
    )
    for c in place_copies:
        c.start()
    edge = HUBER_EDGE
    inv = 1.0 / scale[...]
    row_eff[...] = jnp.zeros_like(row_eff)
    col_eff[...] = jnp.zeros_like(col_eff)
    for sweep in range(SWEEPS):
        row_buf = (row_buf0, row_buf1)[min(sweep, 1)]
        col_buf = (col_buf0, col_buf1)[min(sweep, 1)]

        def clipped(r):
            value = (obs[r] - row_eff[pl.ds(r, 1)] - col_eff[...]) * inv
            return weight[r] * jnp.clip(value, -edge, edge)

        def row_step(r, carry):
            row_buf[0, pl.ds(r, 1)] = jnp.sum(clipped(r), axis=0, keepdims=True)
            if sweep == 0:
                row_buf[0, pl.ds(rows + r, 1)] = jnp.sum(weight[r], axis=0, keepdims=True)
            return carry

        lax.fori_loop(0, rows, row_step, 0)
        total = all_sum(row_buf, "wide", nw, sems_s.at[sweep], sems_r.at[sweep])
        if sweep == 0:
            row_cnt[...] = jnp.maximum(total[rows:], 1.0)
        row_eff[...] = row_eff[...] + scale[...] * total[:rows] / row_cnt[...]

        def col_step(r, carry):
            return carry + clipped(r)

        part = lax.fori_loop(0, rows, col_step, jnp.zeros((cols, lanes), jnp.float32))

        def packed(x):
            x = fold(x)
            low, high = x[:half], x[half:]
            return jnp.where(halves(low, fields), low, high)

        def unpacked(y):
            z = swap(y)
            first = halves(y, fields)
            return jnp.concatenate([jnp.where(first, y, z), jnp.where(first, z, y)], axis=0)

        col_buf[0, pl.ds(0, half)] = packed(part)
        if sweep == 0:
            count = lax.fori_loop(
                0, rows, lambda r, c: c + weight[r], jnp.zeros((cols, lanes), jnp.float32)
            )
            col_buf[0, pl.ds(half, half)] = packed(count)
        total = all_sum(col_buf, "sixteen", ns, sems_s.at[2 + sweep], sems_r.at[2 + sweep])
        if sweep == 0:
            col_cnt[...] = jnp.maximum(unpacked(total[half:]), 1.0)
        col_eff[...] = col_eff[...] + scale[...] * unpacked(total[:half]) / col_cnt[...]

    def rest(r, carry):
        value = weight[r] * (obs[r] - row_eff[pl.ds(r, 1)] - col_eff[...])
        halo[reach + r] = value
        return carry + jnp.sum(value * value, axis=0, keepdims=True)

    squares = lax.fori_loop(0, rows, rest, jnp.zeros((1, lanes), jnp.float32))
    copies = halo_copies(halo, rows, reach, ns, sems_s.at[7], sems_r.at[7])
    for c in copies:
        c.start()
    norm_w[0] = fold(squares)
    norm_s[0] = all_sum(norm_w, "wide", nw, sems_s.at[4], sems_r.at[4])
    norm[...] = all_sum(norm_s, "sixteen", ns, sems_s.at[5], sems_r.at[5])
    for c in copies + place_copies:
        c.wait()


def middle_kernel(
    nw, ns, reach,
    halo_in, image, dots, norm, halo, residual, alpha_out, beta_out, norm_out,
    dot_w, dot_s, norm_w, norm_s, sems_s, sems_r,
):
    rows = image.shape[0]
    lanes = image.shape[2]
    greet((("wide", nw), ("sixteen", ns)))
    dot_w[0] = fold(dots[...])
    dot_s[0] = all_sum(dot_w, "wide", nw, sems_s.at[0], sems_r.at[0])
    alpha = norm[...] / all_sum(dot_s, "sixteen", ns, sems_s.at[1], sems_r.at[1])

    def step(r, carry):
        value = halo_in[reach + r] - alpha * image[r]
        residual[r] = value
        return carry + jnp.sum(value * value, axis=0, keepdims=True)

    squares = lax.fori_loop(0, rows, step, jnp.zeros((1, lanes), jnp.float32))
    norm_w[0] = fold(squares)
    norm_s[0] = all_sum(norm_w, "wide", nw, sems_s.at[2], sems_r.at[2])
    norm_next = all_sum(norm_s, "sixteen", ns, sems_s.at[3], sems_r.at[3])
    beta = norm_next / norm[...]

    def direct(r, carry):
        halo[reach + r] = residual[r] + beta * halo_in[reach + r]
        return carry

    lax.fori_loop(0, rows, direct, 0)
    copies = halo_copies(halo, rows, reach, ns, sems_s.at[4], sems_r.at[4])
    for c in copies:
        c.start()
    alpha_out[...] = alpha
    beta_out[...] = beta
    norm_out[...] = norm_next
    for c in copies:
        c.wait()


def last_kernel(nw, ns, dots, norm, alpha_out, dot_w, dot_s, sems_s, sems_r):
    greet((("wide", nw), ("sixteen", ns)))
    dot_w[0] = fold(dots[...])
    dot_s[0] = all_sum(dot_w, "wide", nw, sems_s.at[0], sems_r.at[0])
    alpha_out[...] = norm[...] / all_sum(dot_s, "sixteen", ns, sems_s.at[1], sems_r.at[1])


def build_windows(halo, windows, starts, span, fields, strip_rows):
    blocks = windows.shape[1]
    pairs = strip_rows // 2

    def one(h, carry):
        for pair in range(pairs):
            for i, start in enumerate(starts):
                x = halo[h * pairs + pair, start : start + span, :]
                first = halves(x, fields)
                z = swap(x)
                for parity in range(2):
                    y = jnp.where(first, x, z) if parity == 0 else jnp.where(first, z, x)
                    high = y.astype(jnp.bfloat16).astype(jnp.float32)
                    both = jnp.where(first, high, y - high).astype(jnp.bfloat16)
                    at = (2 * pair + parity) * span
                    windows[i, h, at : at + span, :] = both
        return carry

    lax.fori_loop(0, blocks, one, 0)


def finish(i, acc, g, halo, image, dots, reach, fields, strip_rows):
    rows = strip_rows * GROUP
    y = fold(acc[:rows] + acc[rows:])
    pairs = strip_rows // 2
    at = pl.multiple_of(i * GROUP, GROUP)
    for pair in range(pairs):
        even = y[(2 * pair) * GROUP : (2 * pair + 1) * GROUP]
        odd = y[(2 * pair + 1) * GROUP : (2 * pair + 2) * GROUP]
        own = halo[reach + g * pairs + pair, pl.ds(at, GROUP), :]
        value = NUGGET_TERM * own + jnp.where(halves(even, fields), even, odd)
        image[pair, pl.ds(at, GROUP), :] = value
        dots[...] += jnp.sum(own * value, axis=0, keepdims=True)


def first_image_kernel(
    starts, span, reach, fields, strip_rows,
    offs, halo, others, centre, tiles, image, dots, windows,
):
    g = pl.program_id(0)
    spread = 2.0 * strip_rows
    cutoff = 6.0 * strip_rows
    wide = strip_rows * span
    rows = strip_rows * GROUP

    @pl.when(g == 0)
    def _():
        build_windows(halo, windows, starts, span, fields, strip_rows)
        dots[...] = jnp.zeros_like(dots)

    def one(i, carry):
        row_here = jnp.broadcast_to(centre[0, i, :, 0:1], (rows, wide))
        col_here = jnp.broadcast_to(centre[0, i, :, 1:2], (rows, wide))
        acc = jnp.zeros((2 * rows, 2 * fields), jnp.float32)
        for n in range(NEIGHBOURS + 1):
            h = g + REACH + offs[n]
            pair = others[h, i]
            row_gap = pair[0:1] - row_here
            col_gap = pair[1:2] - col_here
            square = row_gap * row_gap + col_gap * col_gap
            distance = square * lax.rsqrt(jnp.maximum(square, 1e-30))
            fading = jnp.maximum(1.0 - distance * (1.0 / cutoff), 0.0)
            fading = fading * fading
            fading = fading * fading
            decay = jnp.exp2(distance * (-ROOT_THREE * LOG2E / spread))
            weight = SILL_TERM * (NEIGHBOURS + 1.0 if n == 0 else 1.0)
            lead = weight * (ROOT_THREE / spread) * distance + weight
            kernel = lead * decay * fading * (1.0 + distance * (4.0 / cutoff))
            high = kernel.astype(jnp.bfloat16)
            low = (kernel - high.astype(jnp.float32)).astype(jnp.bfloat16)
            both = jnp.concatenate([high, low], axis=0)
            tiles[0, i, :, n * wide : (n + 1) * wide] = both
            acc = acc + jnp.dot(both, windows[i, h], preferred_element_type=jnp.float32)
        finish(i, acc, g, halo, image, dots, reach, fields, strip_rows)
        return carry

    lax.fori_loop(0, len(starts), one, 0)


def second_image_kernel(
    starts, span, reach, fields, strip_rows,
    offs, halo, tiles, image, dots, windows,
):
    g = pl.program_id(0)
    wide = strip_rows * span
    rows = strip_rows * GROUP

    @pl.when(g == 0)
    def _():
        build_windows(halo, windows, starts, span, fields, strip_rows)
        dots[...] = jnp.zeros_like(dots)

    def one(i, carry):
        acc = jnp.zeros((2 * rows, 2 * fields), jnp.float32)
        for n in range(NEIGHBOURS + 1):
            h = g + REACH + offs[n]
            acc = acc + jnp.dot(
                tiles[0, i, :, n * wide : (n + 1) * wide],
                windows[i, h],
                preferred_element_type=jnp.float32,
            )
        finish(i, acc, g, halo, image, dots, reach, fields, strip_rows)
        return carry

    lax.fori_loop(0, len(starts), one, 0)


def on_device(observations, huber_scale, observed, jitter, owner_map, neighbours):
    fields, row_dev, col_dev = observations.shape
    nw, ns = lax.axis_size("wide"), lax.axis_size("sixteen")
    my_place = lax.axis_index("sixteen")
    group_place = lax.axis_index("wide")
    strip_rows = BLOCK // col_dev
    total_strips = BLOCKS_DEV * ns
    rows, lanes = row_dev // 2, 2 * fields
    pairs = strip_rows // 2
    reach = REACH * pairs
    f32 = jnp.float32
    shape = jax.ShapeDtypeStruct

    def pack(x):
        return x.reshape(fields, rows, 2, col_dev).transpose(1, 3, 2, 0).reshape(rows, col_dev, lanes)

    obs = pack(observations)
    weight = pack(jnp.broadcast_to(observed.astype(f32)[None], observations.shape))
    scale = jnp.concatenate([huber_scale, huber_scale])[None]
    row_place = (my_place * row_dev + jnp.arange(row_dev, dtype=jnp.int32)).astype(f32)
    col_place = (group_place * col_dev + jnp.arange(col_dev, dtype=jnp.int32)).astype(f32)
    place = jnp.stack(
        [row_place[:, None] + jitter[0], col_place[None, :] + jitter[1]], axis=1
    )
    most = max(nw, ns)
    halo, place_halo, norm = pl.pallas_call(
        functools.partial(polish_kernel, nw, ns, fields, reach),
        out_shape=(
            shape((rows + 2 * reach, col_dev, lanes), f32),
            shape((row_dev + 4 * reach, 2, col_dev), f32),
            shape((1, lanes), f32),
        ),
        in_specs=[VMEM] * 4,
        out_specs=(VMEM,) * 3,
        scratch_shapes=[
            pltpu.VMEM((rows, lanes), f32),
            pltpu.VMEM((rows, lanes), f32),
            pltpu.VMEM((col_dev, lanes), f32),
            pltpu.VMEM((col_dev, lanes), f32),
            pltpu.VMEM((nw, 2 * rows, lanes), f32),
            pltpu.VMEM((nw, rows, lanes), f32),
            pltpu.VMEM((ns, col_dev, lanes), f32),
            pltpu.VMEM((ns, col_dev // 2, lanes), f32),
            pltpu.VMEM((nw, 1, lanes), f32),
            pltpu.VMEM((ns, 1, lanes), f32),
            pltpu.SemaphoreType.DMA((8, most)),
            pltpu.SemaphoreType.DMA((8, most)),
        ],
        compiler_params=pltpu.CompilerParams(collective_id=0, has_side_effects=True),
    )(obs, weight, scale, place)

    cut = 6 * strip_rows
    span = GROUP + 2 * cut
    starts = tuple(
        min(max(GROUP * i - cut, 0), col_dev - span) for i in range(col_dev // GROUP)
    )
    groups = len(starts)
    wide = strip_rows * span
    blocks_halo = BLOCKS_DEV + 2 * REACH
    by_block = place_halo.reshape(blocks_halo, strip_rows, 2, col_dev)
    others = jnp.stack([by_block[..., s : s + span] for s in starts], axis=1)
    others = others.transpose(0, 1, 3, 2, 4).reshape(blocks_halo, groups, 2, wide)
    centre = place.reshape(BLOCKS_DEV, strip_rows, 2, groups, GROUP)
    centre = centre.transpose(0, 3, 1, 4, 2).reshape(BLOCKS_DEV, groups, strip_rows * GROUP, 2)
    listed = (neighbours[0, 0] + total_strips // 2) % total_strips - total_strips // 2
    offs = jnp.concatenate([jnp.zeros((1,), jnp.int32), listed])

    tile_block = (1, groups, 2 * strip_rows * GROUP, (NEIGHBOURS + 1) * wide)
    tile_shape = shape((BLOCKS_DEV,) + tile_block[1:], jnp.bfloat16)
    macs = BLOCKS_DEV * groups * tile_block[2] * tile_block[3]
    whole_halo = pl.BlockSpec((rows + 2 * reach, col_dev, lanes), lambda g: (0, 0, 0))
    tile_spec = pl.BlockSpec(tile_block, lambda g: (g, 0, 0, 0))
    image_spec = pl.BlockSpec((pairs, col_dev, lanes), lambda g: (g, 0, 0))
    dots_spec = pl.BlockSpec((1, lanes), lambda g: (0, 0))
    image_shape = shape((rows, col_dev, lanes), f32)
    dots_shape = shape((1, lanes), f32)
    window_scratch = pltpu.VMEM((groups, blocks_halo, wide, lanes), jnp.bfloat16)
    static = (starts, span, reach, fields, strip_rows)
    tiles, image, dots = pl.pallas_call(
        functools.partial(first_image_kernel, *static),
        grid=(BLOCKS_DEV,),
        out_shape=(tile_shape, image_shape, dots_shape),
        in_specs=[
            SMEM,
            whole_halo,
            pl.BlockSpec((blocks_halo, groups, 2, wide), lambda g: (0, 0, 0, 0)),
            pl.BlockSpec((1, groups, strip_rows * GROUP, 2), lambda g: (g, 0, 0, 0)),
        ],
        out_specs=(tile_spec, image_spec, dots_spec),
        scratch_shapes=[window_scratch],
        cost_estimate=pl.CostEstimate(
            flops=macs * 256, bytes_accessed=macs * 2, transcendentals=macs
        ),
    )(offs, halo, others, centre)

    def mid(name_id, kernel, args, out_shape, phases, extra):
        return pl.pallas_call(
            kernel,
            out_shape=out_shape,
            in_specs=[VMEM] * len(args),
            out_specs=(VMEM,) * len(out_shape),
            scratch_shapes=[pltpu.VMEM((n, 1, lanes), f32) for _ in range(extra) for n in (nw, ns)]
            + [pltpu.SemaphoreType.DMA((phases, most))] * 2,
            compiler_params=pltpu.CompilerParams(collective_id=name_id, has_side_effects=True),
        )(*args)

    halo1, residual, alpha0, beta, norm1 = mid(
        1,
        functools.partial(middle_kernel, nw, ns, reach),
        (halo, image, dots, norm),
        (shape(halo.shape, f32), image_shape, dots_shape, dots_shape, dots_shape),
        5,
        2,
    )
    image1, dots1 = pl.pallas_call(
        functools.partial(second_image_kernel, *static),
        grid=(BLOCKS_DEV,),
        out_shape=(image_shape, dots_shape),
        in_specs=[SMEM, whole_halo, tile_spec],
        out_specs=(image_spec, dots_spec),
        scratch_shapes=[window_scratch],
        cost_estimate=pl.CostEstimate(
            flops=macs * 256, bytes_accessed=macs * 2, transcendentals=0
        ),
    )(offs, halo1, tiles)
    (alpha1,) = mid(
        2, functools.partial(last_kernel, nw, ns), (dots1, norm1), (dots_shape,), 2, 1
    )

    group_map = owner_map[0]
    table = owned_table(group_map, ns, BLOCKS_DEV)
    my_ids = lax.dynamic_index_in_dim(table, my_place, 0, keepdims=False)
    my_targets = lax.dynamic_slice_in_dim(group_map, my_place * BLOCKS_DEV, BLOCKS_DEV)
    hit = my_targets[None, :] == jnp.arange(ns, dtype=jnp.int32)[:, None]
    order = jnp.sum(hit * jnp.arange(BLOCKS_DEV, dtype=jnp.int32)[None], axis=1, dtype=jnp.int32)
    sources = my_ids // BLOCKS_DEV

    def moved(x):
        out = jnp.take(x.reshape(BLOCKS_DEV, pairs * col_dev, lanes), order, axis=0)
        got = lax.all_to_all(out, "sixteen", split_axis=0, concat_axis=0, tiled=True)
        got = jnp.take(got, sources, axis=0)
        return got.reshape(BLOCKS_DEV, pairs, col_dev, lanes)

    def unpack(x):
        x = x.reshape(BLOCKS_DEV, pairs, col_dev, 2, fields).transpose(4, 0, 1, 3, 2)
        return x.reshape(1, 1, fields, BLOCKS_DEV, BLOCK)

    start, mid_residual, last_image = (
        moved(halo[reach : reach + rows]), moved(residual), moved(image1)
    )
    solution_now = (alpha0 + alpha1 * beta) * start + alpha1 * mid_residual
    residual_now = mid_residual - alpha1 * last_image
    return unpack(solution_now), unpack(residual_now)


def solution(mesh):
    return jax.shard_map(
        on_device,
        mesh=mesh,
        in_specs=(
            P(None, "sixteen", "wide"),
            P(),
            P("sixteen", "wide"),
            P(None, "sixteen", "wide"),
            P("wide", None),
            P("wide", None, None),
        ),
        out_specs=(P("wide", "sixteen", None, None, None), P("wide", "sixteen", None, None, None)),
        check_vma=False,
    )
```

```python
import functools

import jax
import jax.numpy as jnp
from jax import lax
from jax.experimental import pallas as pl
from jax.experimental.pallas import tpu as pltpu
from jax.sharding import PartitionSpec as P

BLOCK = 512
BLOCKS_DEV = 8
REACH = 4
NEIGHBOURS = 6
SWEEPS = 2

HUBER_EDGE = 1.345
NUGGET_TERM = 1.0
SILL_TERM = 0.02
ROOT_THREE = 1.7320508075688772
LOG2E = 1.4426950408889634
GROUP = 16
MESH = pl.DeviceIdType.MESH
VMEM = pl.BlockSpec(memory_space=pltpu.VMEM)
SMEM = pl.BlockSpec(memory_space=pltpu.SMEM)


def owned_table(group_map, owners, per_owner):
    total_strips = group_map.shape[0]
    member = (group_map[None, :] == jnp.arange(owners, dtype=jnp.int32)[:, None]).astype(jnp.int32)
    ranked = jnp.cumsum(member, axis=1, dtype=jnp.int32) - 1
    slot_hit = (ranked[:, :, None] == jnp.arange(per_owner, dtype=jnp.int32)[None, None, :]).astype(
        jnp.int32
    ) * member[:, :, None]
    numbers = jnp.arange(total_strips, dtype=jnp.int32)
    return jnp.sum(slot_hit * numbers[None, :, None], axis=1, dtype=jnp.int32)


def greet(sizes):
    barrier = pltpu.get_barrier_semaphore()
    for axis, n in sizes:
        me = lax.axis_index(axis)

        def say(k, carry, axis=axis, n=n, me=me):
            pl.semaphore_signal(
                barrier, inc=1, device_id={axis: lax.rem(me + k, n)}, device_id_type=MESH
            )
            return carry

        lax.fori_loop(1, n, say, 0)
    pl.semaphore_wait(barrier, sum(n - 1 for _, n in sizes))


def all_sum(buffer, axis, n, send_sem, recv_sem):
    me = lax.axis_index(axis)

    def copy(k):
        return pltpu.make_async_remote_copy(
            src_ref=buffer.at[0],
            dst_ref=buffer.at[k],
            send_sem=send_sem.at[k],
            recv_sem=recv_sem.at[k],
            device_id={axis: lax.rem(me + k, n)},
            device_id_type=MESH,
        )

    copies = [copy(k) for k in range(1, n)]
    for c in copies:
        c.start()
    for c in copies:
        c.wait()
    total = None
    for owner in range(n):
        term = buffer[lax.rem(me - owner + n, n)]
        total = term if total is None else total + term
    return total


def swap(x):
    return pltpu.roll(x, x.shape[-1] // 2, x.ndim - 1)


def fold(x):
    return x + swap(x)


def halves(x, fields):
    return lax.broadcasted_iota(jnp.int32, x.shape, x.ndim - 1) < fields


def halo_copies(halo, rows, reach, n, send_sem, recv_sem, axis="sixteen"):
    me = lax.axis_index(axis)
    up, down = lax.rem(me + 1, n), lax.rem(me + n - 1, n)
    return [
        pltpu.make_async_remote_copy(
            src_ref=halo.at[pl.ds(rows, reach)],
            dst_ref=halo.at[pl.ds(0, reach)],
            send_sem=send_sem.at[0],
            recv_sem=recv_sem.at[0],
            device_id={axis: up},
            device_id_type=MESH,
        ),
        pltpu.make_async_remote_copy(
            src_ref=halo.at[pl.ds(reach, reach)],
            dst_ref=halo.at[pl.ds(reach + rows, reach)],
            send_sem=send_sem.at[1],
            recv_sem=recv_sem.at[1],
            device_id={axis: down},
            device_id_type=MESH,
        ),
    ]


def polish_kernel(
    nw, ns, fields, reach,
    obs, weight, scale, place, halo, place_halo, norm,
    row_eff, row_cnt, col_eff, col_cnt,
    row_buf0, row_buf1, col_buf0, col_buf1, norm_w, norm_s,
    sems_s, sems_r,
):
    rows, cols, lanes = obs.shape
    half = cols // 2
    place_rows = place.shape[0]
    place_reach = 2 * reach
    greet((("wide", nw), ("sixteen", ns)))
    place_halo[pl.ds(place_reach, place_rows)] = place[...]
    place_copies = halo_copies(
        place_halo, place_rows, place_reach, ns, sems_s.at[6], sems_r.at[6]
    )
    for c in place_copies:
        c.start()
    edge = HUBER_EDGE
    diagonal = lax.broadcasted_iota(jnp.int32, (cols, lanes), 0) == lax.broadcasted_iota(
        jnp.int32, (cols, lanes), 1
    )
    inv = 1.0 / scale[...]
    row_eff[...] = jnp.zeros_like(row_eff)
    col_eff[...] = jnp.zeros_like(col_eff)
    for sweep in range(SWEEPS):
        row_buf = (row_buf0, row_buf1)[min(sweep, 1)]
        col_buf = (col_buf0, col_buf1)[min(sweep, 1)]

        def clipped(r):
            value = (obs[r] - row_eff[pl.ds(r, 1)] - col_eff[...]) * inv
            return weight[r] * jnp.clip(value, -edge, edge)

        def row_step(r, carry):
            row_buf[0, pl.ds(r, 1)] = jnp.sum(clipped(r), axis=0, keepdims=True)
            if sweep == 0:
                row_buf[0, pl.ds(rows + r, 1)] = jnp.sum(weight[r], axis=0, keepdims=True)
            return carry

        lax.fori_loop(0, rows, row_step, 0)
        total = all_sum(row_buf, "wide", nw, sems_s.at[sweep], sems_r.at[sweep])
        if sweep == 0:
            row_cnt[...] = jnp.maximum(total[rows:], 1.0)
        row_eff[...] = row_eff[...] + scale[...] * total[:rows] / row_cnt[...]

        def col_step(r, carry):
            return carry + clipped(r)

        part = lax.fori_loop(0, rows, col_step, jnp.zeros((cols, lanes), jnp.float32))

        def packed(x):
            x = fold(x)
            low, high = x[:half], x[half:]
            return jnp.where(halves(low, fields), low, high)

        def unpacked(y):
            z = swap(y)
            first = halves(y, fields)
            return jnp.concatenate([jnp.where(first, y, z), jnp.where(first, z, y)], axis=0)

        col_buf[0, pl.ds(0, half)] = packed(part)
        if sweep == 0:
            col_buf[0, pl.ds(half, 8)] = jnp.zeros((8, lanes), jnp.float32)
            count = lax.fori_loop(
                0, rows, lambda r, c: c + weight[r], jnp.zeros((cols, lanes), jnp.float32)
            )
            col_buf[0, pl.ds(half, 1)] = jnp.sum(
                jnp.where(diagonal, fold(count), 0.0), axis=0, keepdims=True
            )
        total = all_sum(col_buf, "sixteen", ns, sems_s.at[2 + sweep], sems_r.at[2 + sweep])
        if sweep == 0:
            spread = jnp.where(diagonal, jnp.broadcast_to(total[half : half + 1], (cols, lanes)), 0.0)
            count = jnp.sum(spread, axis=1, keepdims=True)
            col_cnt[...] = jnp.maximum(jnp.broadcast_to(count, (cols, lanes)), 1.0)
        col_eff[...] = col_eff[...] + scale[...] * unpacked(total[:half]) / col_cnt[...]

    def rest(r, carry):
        value = weight[r] * (obs[r] - row_eff[pl.ds(r, 1)] - col_eff[...])
        halo[reach + r] = value
        return carry + jnp.sum(value * value, axis=0, keepdims=True)

    squares = lax.fori_loop(0, rows, rest, jnp.zeros((1, lanes), jnp.float32))
    copies = halo_copies(halo, rows, reach, ns, sems_s.at[7], sems_r.at[7])
    for c in copies:
        c.start()
    norm_w[0] = fold(squares)
    norm_s[0] = all_sum(norm_w, "wide", nw, sems_s.at[4], sems_r.at[4])
    norm[...] = all_sum(norm_s, "sixteen", ns, sems_s.at[5], sems_r.at[5])
    for c in copies + place_copies:
        c.wait()


def middle_kernel(
    nw, ns, reach,
    row_map, halo_in, image, dots, norm, halo, residual, alpha_out, beta_out, norm_out,
    dot_w, dot_s, norm_w, norm_s, sems_s, sems_r,
):
    rows = image.shape[0]
    lanes = image.shape[2]
    greet((("wide", nw), ("sixteen", ns)))
    dot_w[0] = fold(dots[...])
    dot_s[0] = all_sum(dot_w, "wide", nw, sems_s.at[0], sems_r.at[0])
    alpha = norm[...] / all_sum(dot_s, "sixteen", ns, sems_s.at[1], sems_r.at[1])

    def step(r, carry):
        value = halo_in[reach + r] - alpha * image[row_map[r]]
        residual[r] = value
        return carry + jnp.sum(value * value, axis=0, keepdims=True)

    squares = lax.fori_loop(0, rows, step, jnp.zeros((1, lanes), jnp.float32))
    norm_w[0] = fold(squares)
    norm_s[0] = all_sum(norm_w, "wide", nw, sems_s.at[2], sems_r.at[2])
    norm_next = all_sum(norm_s, "sixteen", ns, sems_s.at[3], sems_r.at[3])
    beta = norm_next / norm[...]

    def direct(r, carry):
        halo[reach + r] = residual[r] + beta * halo_in[reach + r]
        return carry

    lax.fori_loop(0, rows, direct, 0)
    copies = halo_copies(halo, rows, reach, ns, sems_s.at[4], sems_r.at[4])
    for c in copies:
        c.start()
    alpha_out[...] = alpha
    beta_out[...] = beta
    norm_out[...] = norm_next
    for c in copies:
        c.wait()


def build_windows(halo, windows, starts, span, fields, strip_rows):
    blocks = windows.shape[1]
    pairs = strip_rows // 2

    def one(h, carry):
        for pair in range(pairs):
            for i, start in enumerate(starts):
                x = halo[h * pairs + pair, start : start + span, :]
                first = halves(x, fields)
                z = swap(x)
                for parity in range(2):
                    y = jnp.where(first, x, z) if parity == 0 else jnp.where(first, z, x)
                    high = y.astype(jnp.bfloat16).astype(jnp.float32)
                    both = jnp.where(first, high, y - high).astype(jnp.bfloat16)
                    at = (2 * pair + parity) * span
                    windows[i, h, at : at + span, :] = both
        return carry

    lax.fori_loop(0, blocks, one, 0)


def finish(i, acc, own_of, store, dots, fields, strip_rows):
    rows = strip_rows * GROUP
    y = fold(acc[:rows] + acc[rows:])
    at = pl.multiple_of(i * GROUP, GROUP)
    for pair in range(strip_rows // 2):
        even = y[(2 * pair) * GROUP : (2 * pair + 1) * GROUP]
        odd = y[(2 * pair + 1) * GROUP : (2 * pair + 2) * GROUP]
        own = own_of(pair, at)
        value = NUGGET_TERM * own + jnp.where(halves(even, fields), even, odd)
        store(pair, at, value)
        dots[...] += jnp.sum(own * value, axis=0, keepdims=True)


def shifted(staged, received, n, send_sem, recv_sem):
    me = lax.axis_index("sixteen")
    return [pltpu.make_async_copy(staged.at[0], received.at[0], send_sem.at[0])] + [
        pltpu.make_async_remote_copy(
            src_ref=staged.at[k],
            dst_ref=received.at[k],
            send_sem=send_sem.at[k],
            recv_sem=recv_sem.at[k],
            device_id={"sixteen": lax.rem(me + k, n)},
            device_id_type=MESH,
        )
        for k in range(1, n)
    ]


def stage(staged, source, first, chosen):
    slots, pairs = staged.shape[:2]

    def one(k, carry):
        for pair in range(pairs):
            staged[k, pair] = source[first + chosen[k] * pairs + pair]
        return carry

    lax.fori_loop(0, slots, one, 0)


def first_image_kernel(
    ns, starts, span, reach, fields, strip_rows,
    offs, step_block, chosen, halo, others, centre,
    tiles, image, dots, received,
    windows, staged, send_sem, recv_sem,
):
    g = pl.program_id(0)
    pairs = strip_rows // 2
    spread = 2.0 * strip_rows
    cutoff = 6.0 * strip_rows
    wide = strip_rows * span
    rows = strip_rows * GROUP

    @pl.when(g == 0)
    def _():
        stage(staged, halo, reach, chosen)
        greet((("sixteen", ns),))
        for c in shifted(staged, received, ns, send_sem, recv_sem):
            c.start()
        build_windows(halo, windows, starts, span, fields, strip_rows)
        dots[...] = jnp.zeros_like(dots)

    block = step_block[g]

    def one(i, carry):
        here = centre[block, i]
        row_here = jnp.broadcast_to(here[:, 0:1], (rows, wide))
        col_here = jnp.broadcast_to(here[:, 1:2], (rows, wide))
        acc = jnp.zeros((2 * rows, 2 * fields), jnp.float32)
        for n in range(NEIGHBOURS + 1):
            h = block + REACH + offs[n]
            pair = others[h, i]
            row_gap = pair[0:1] - row_here
            col_gap = pair[1:2] - col_here
            square = row_gap * row_gap + col_gap * col_gap
            distance = square * lax.rsqrt(jnp.maximum(square, 1e-30))
            fading = jnp.maximum(1.0 - distance * (1.0 / cutoff), 0.0)
            fading = fading * fading
            fading = fading * fading
            decay = jnp.exp2(distance * (-ROOT_THREE * LOG2E / spread))
            weight = SILL_TERM * (NEIGHBOURS + 1.0 if n == 0 else 1.0)
            lead = weight * (ROOT_THREE / spread) * distance + weight
            kernel = lead * decay * fading * (1.0 + distance * (4.0 / cutoff))
            high = kernel.astype(jnp.bfloat16)
            low = (kernel - high.astype(jnp.float32)).astype(jnp.bfloat16)
            both = jnp.concatenate([high, low], axis=0)
            tiles[0, i, :, n * wide : (n + 1) * wide] = both
            acc = acc + jnp.dot(both, windows[i, h], preferred_element_type=jnp.float32)

        def store(pair, at, value):
            image[pair, pl.ds(at, GROUP), :] = value

        def own_of(pair, at):
            return halo[reach + block * pairs + pair, pl.ds(at, GROUP), :]

        finish(i, acc, own_of, store, dots, fields, strip_rows)
        return carry

    lax.fori_loop(0, len(starts), one, 0)

    @pl.when(g == pl.num_programs(0) - 1)
    def _():
        for c in shifted(staged, received, ns, send_sem, recv_sem):
            c.wait()


def second_image_kernel(
    nw, ns, starts, span, reach, fields, strip_rows,
    offs, step_block, chosen, halo, residual, norm, tiles,
    alpha, received_residual, received_image,
    windows, dots, staged, staged_image, local_image, dot_w, dot_s,
    send_sem, recv_sem, send_image, recv_image, sems_s, sems_r,
):
    g = pl.program_id(0)
    last = pl.num_programs(0) - 1
    pairs = strip_rows // 2
    wide = strip_rows * span
    rows = strip_rows * GROUP
    by_owner = ns == BLOCKS_DEV

    @pl.when(g == 0)
    def _():
        stage(staged, residual, 0, chosen)
        greet((("wide", nw), ("sixteen", ns)))
        for c in shifted(staged, received_residual, ns, send_sem, recv_sem):
            c.start()
        build_windows(halo, windows, starts, span, fields, strip_rows)
        dots[...] = jnp.zeros_like(dots)

    block = step_block[g]
    slot = lax.rem(g + 1, BLOCKS_DEV) if by_owner else g

    def one(i, carry):
        acc = jnp.zeros((2 * rows, 2 * fields), jnp.float32)
        for n in range(NEIGHBOURS + 1):
            h = block + REACH + offs[n]
            acc = acc + jnp.dot(
                tiles[0, i, :, n * wide : (n + 1) * wide],
                windows[i, h],
                preferred_element_type=jnp.float32,
            )

        def store(pair, at, value):
            if by_owner:
                staged_image[slot, pair, pl.ds(at, GROUP), :] = value
            else:
                local_image[slot * pairs + pair, pl.ds(at, GROUP), :] = value

        def own_of(pair, at):
            return halo[reach + block * pairs + pair, pl.ds(at, GROUP), :]

        finish(i, acc, own_of, store, dots, fields, strip_rows)
        return carry

    lax.fori_loop(0, len(starts), one, 0)
    images = shifted(staged_image, received_image, ns, send_image, recv_image)
    if by_owner:
        for k in range(ns):

            @pl.when(g == (k - 1) % ns)
            def _(k=k):
                images[k].start()

    @pl.when(g == last)
    def _():
        if not by_owner:
            stage(staged_image, local_image, 0, chosen)
            for c in images:
                c.start()
        dot_w[0] = fold(dots[...])
        dot_s[0] = all_sum(dot_w, "wide", nw, sems_s.at[0], sems_r.at[0])
        alpha[...] = norm[...] / all_sum(dot_s, "sixteen", ns, sems_s.at[1], sems_r.at[1])
        for c in shifted(staged, received_residual, ns, send_sem, recv_sem):
            c.wait()
        for c in images:
            c.wait()


def final_kernel(fields, strip_rows, came, start, residual, image, alpha0, alpha1, beta, out, rest):
    pairs, cols = start.shape[1:3]
    lead = alpha0[...] + alpha1[...] * beta[...]
    step = alpha1[...]
    for j in range(BLOCKS_DEV):
        k = came[j]
        for pair in range(pairs):
            value = residual[k, pair]
            first = (lead * start[k, pair] + step * value).T
            second = (value - step * image[k, pair]).T
            for parity in range(2):
                at = (2 * pair + parity) * cols
                part = slice(parity * fields, (parity + 1) * fields)
                out[:, j, at : at + cols] = first[part]
                rest[:, j, at : at + cols] = second[part]


def on_device(observations, huber_scale, observed, jitter, owner_map, neighbours):
    fields, row_dev, col_dev = observations.shape
    nw, ns = lax.axis_size("wide"), lax.axis_size("sixteen")
    my_place = lax.axis_index("sixteen")
    group_place = lax.axis_index("wide")
    strip_rows = BLOCK // col_dev
    total_strips = BLOCKS_DEV * ns
    rows, lanes = row_dev // 2, 2 * fields
    pairs = strip_rows // 2
    reach = REACH * pairs
    f32 = jnp.float32
    shape = jax.ShapeDtypeStruct

    def pack(x):
        return x.reshape(fields, rows, 2, col_dev).transpose(1, 3, 2, 0).reshape(rows, col_dev, lanes)

    obs = pack(observations)
    weight = pack(jnp.broadcast_to(observed.astype(f32)[None], observations.shape))
    scale = jnp.concatenate([huber_scale, huber_scale])[None]
    row_place = (my_place * row_dev + jnp.arange(row_dev, dtype=jnp.int32)).astype(f32)
    col_place = (group_place * col_dev + jnp.arange(col_dev, dtype=jnp.int32)).astype(f32)
    place = jnp.stack(
        [row_place[:, None] + jitter[0], col_place[None, :] + jitter[1]], axis=1
    )
    most = max(nw, ns)
    halo, place_halo, norm = pl.pallas_call(
        functools.partial(polish_kernel, nw, ns, fields, reach),
        out_shape=(
            shape((rows + 2 * reach, col_dev, lanes), f32),
            shape((row_dev + 4 * reach, 2, col_dev), f32),
            shape((1, lanes), f32),
        ),
        in_specs=[VMEM] * 4,
        out_specs=(VMEM,) * 3,
        scratch_shapes=[
            pltpu.VMEM((rows, lanes), f32),
            pltpu.VMEM((rows, lanes), f32),
            pltpu.VMEM((col_dev, lanes), f32),
            pltpu.VMEM((col_dev, lanes), f32),
            pltpu.VMEM((nw, 2 * rows, lanes), f32),
            pltpu.VMEM((nw, rows, lanes), f32),
            pltpu.VMEM((ns, col_dev // 2 + 8, lanes), f32),
            pltpu.VMEM((ns, col_dev // 2, lanes), f32),
            pltpu.VMEM((nw, 1, lanes), f32),
            pltpu.VMEM((ns, 1, lanes), f32),
            pltpu.SemaphoreType.DMA((8, most)),
            pltpu.SemaphoreType.DMA((8, most)),
        ],
        compiler_params=pltpu.CompilerParams(collective_id=0, has_side_effects=True),
    )(obs, weight, scale, place)

    cut = 6 * strip_rows
    span = GROUP + 2 * cut
    starts = tuple(
        min(max(GROUP * i - cut, 0), col_dev - span) for i in range(col_dev // GROUP)
    )
    groups = len(starts)
    wide = strip_rows * span
    blocks_halo = BLOCKS_DEV + 2 * REACH
    by_block = place_halo.reshape(blocks_halo, strip_rows, 2, col_dev)
    others = jnp.stack([by_block[..., s : s + span] for s in starts], axis=1)
    others = others.transpose(0, 1, 3, 2, 4).reshape(blocks_halo, groups, 2, wide)
    centre = place.reshape(BLOCKS_DEV, strip_rows, 2, groups, GROUP)
    centre = centre.transpose(0, 3, 1, 4, 2).reshape(BLOCKS_DEV, groups, strip_rows * GROUP, 2)
    listed = (neighbours[0, 0] + total_strips // 2) % total_strips - total_strips // 2
    offs = jnp.concatenate([jnp.zeros((1,), jnp.int32), listed])

    tile_block = (1, groups, 2 * strip_rows * GROUP, (NEIGHBOURS + 1) * wide)
    tile_shape = shape((BLOCKS_DEV,) + tile_block[1:], jnp.bfloat16)
    whole_halo = pl.BlockSpec((rows + 2 * reach, col_dev, lanes), lambda g: (0, 0, 0))
    tile_spec = pl.BlockSpec(tile_block, lambda g: (g, 0, 0, 0))
    image_spec = pl.BlockSpec((pairs, col_dev, lanes), lambda g: (g, 0, 0))
    dots_spec = pl.BlockSpec((1, lanes), lambda g: (0, 0))
    image_shape = shape((rows, col_dev, lanes), f32)
    dots_shape = shape((1, lanes), f32)
    window_scratch = pltpu.VMEM((groups, blocks_halo, wide, lanes), jnp.bfloat16)
    static = (starts, span, reach, fields, strip_rows)
    group_map = owner_map[0]
    numbers = jnp.arange(BLOCKS_DEV, dtype=jnp.int32)
    table = owned_table(group_map, ns, BLOCKS_DEV)
    my_ids = lax.dynamic_index_in_dim(table, my_place, 0, keepdims=False)
    my_targets = lax.dynamic_slice_in_dim(group_map, my_place * BLOCKS_DEV, BLOCKS_DEV)
    owners = (my_place + jnp.arange(ns, dtype=jnp.int32)) % ns
    hit = my_targets[None, :] == owners[:, None]
    chosen = jnp.sum(hit * numbers[None], axis=1, dtype=jnp.int32)
    came = (my_place - my_ids // BLOCKS_DEV + ns) % ns
    if ns == BLOCKS_DEV:
        step_block = jnp.roll(chosen, -1)
        step_of = jnp.sum(
            (step_block[None, :] == numbers[:, None]) * numbers[None], axis=1, dtype=jnp.int32
        )
    else:
        step_block = step_of = numbers
    row_map = (step_of[:, None] * pairs + jnp.arange(pairs, dtype=jnp.int32)[None]).reshape(-1)
    anywhere = pl.BlockSpec(memory_space=pl.ANY)
    moved_shape = shape((ns, pairs, col_dev, lanes), f32)
    staging = pltpu.VMEM(moved_shape.shape, f32)

    tiles, image, dots, start = pl.pallas_call(
        functools.partial(first_image_kernel, ns, *static),
        grid=(BLOCKS_DEV,),
        out_shape=(tile_shape, image_shape, dots_shape, moved_shape),
        in_specs=[
            SMEM,
            SMEM,
            SMEM,
            whole_halo,
            pl.BlockSpec((blocks_halo, groups, 2, wide), lambda g: (0, 0, 0, 0)),
            pl.BlockSpec((BLOCKS_DEV, groups, strip_rows * GROUP, 2), lambda g: (0, 0, 0, 0)),
        ],
        out_specs=(tile_spec, image_spec, dots_spec, anywhere),
        scratch_shapes=[window_scratch, staging] + [pltpu.SemaphoreType.DMA((ns,))] * 2,
        compiler_params=pltpu.CompilerParams(collective_id=3, has_side_effects=True),
    )(offs, step_block, chosen, halo, others, centre)

    def mid(name_id, kernel, args, out_shape, phases, extra):
        return pl.pallas_call(
            kernel,
            out_shape=out_shape,
            in_specs=[SMEM] + [VMEM] * (len(args) - 1),
            out_specs=(VMEM,) * len(out_shape),
            scratch_shapes=[pltpu.VMEM((n, 1, lanes), f32) for _ in range(extra) for n in (nw, ns)]
            + [pltpu.SemaphoreType.DMA((phases, most))] * 2,
            compiler_params=pltpu.CompilerParams(collective_id=name_id, has_side_effects=True),
        )(*args)

    halo1, residual, alpha0, beta, norm1 = mid(
        1,
        functools.partial(middle_kernel, nw, ns, reach),
        (row_map, halo, image, dots, norm),
        (shape(halo.shape, f32), image_shape, dots_shape, dots_shape, dots_shape),
        5,
        2,
    )
    alpha1, mid_residual, last_image = pl.pallas_call(
        functools.partial(second_image_kernel, nw, ns, *static),
        grid=(BLOCKS_DEV,),
        out_shape=(dots_shape, moved_shape, moved_shape),
        in_specs=[
            SMEM,
            SMEM,
            SMEM,
            whole_halo,
            pl.BlockSpec((rows, col_dev, lanes), lambda g: (0, 0, 0)),
            dots_spec,
            tile_spec,
        ],
        out_specs=(dots_spec, anywhere, anywhere),
        scratch_shapes=[
            window_scratch,
            pltpu.VMEM((1, lanes), f32),
            staging,
            staging,
            pltpu.VMEM((8, 128) if ns == BLOCKS_DEV else (rows, col_dev, lanes), f32),
            pltpu.VMEM((nw, 1, lanes), f32),
            pltpu.VMEM((ns, 1, lanes), f32),
        ]
        + [pltpu.SemaphoreType.DMA((ns,))] * 4
        + [pltpu.SemaphoreType.DMA((2, most))] * 2,
        compiler_params=pltpu.CompilerParams(collective_id=2, has_side_effects=True),
    )(offs, step_block, chosen, halo1, residual, norm1, tiles)

    out_shape = shape((fields, BLOCKS_DEV, BLOCK), f32)
    solution_now, residual_now = pl.pallas_call(
        functools.partial(final_kernel, fields, strip_rows),
        out_shape=(out_shape, out_shape),
        in_specs=[SMEM] + [VMEM] * 6,
        out_specs=(VMEM, VMEM),
    )(came, start, mid_residual, last_image, alpha0, alpha1, beta)
    return solution_now[None, None], residual_now[None, None]


def solution(mesh):
    return jax.shard_map(
        on_device,
        mesh=mesh,
        in_specs=(
            P(None, "sixteen", "wide"),
            P(),
            P("sixteen", "wide"),
            P(None, "sixteen", "wide"),
            P("wide", None),
            P("wide", None, None),
        ),
        out_specs=(P("wide", "sixteen", None, None, None), P("wide", "sixteen", None, None, None)),
        check_vma=False,
    )
```

```python
import functools

import jax
import jax.numpy as jnp
from jax import lax
from jax.experimental import pallas as pl
from jax.experimental.pallas import tpu as pltpu
from jax.sharding import PartitionSpec as P

BLOCK = 512
BLOCKS_DEV = 8
REACH = 4
NEIGHBOURS = 6
SWEEPS = 2

HUBER_EDGE = 1.345
NUGGET_TERM = 1.0
SILL_TERM = 0.02
ROOT_THREE = 1.7320508075688772
LOG2E = 1.4426950408889634
GROUP = 16
MESH = pl.DeviceIdType.MESH
VMEM = pl.BlockSpec(memory_space=pltpu.VMEM)
SMEM = pl.BlockSpec(memory_space=pltpu.SMEM)


def owned_table(group_map, owners, per_owner):
    total_strips = group_map.shape[0]
    member = (group_map[None, :] == jnp.arange(owners, dtype=jnp.int32)[:, None]).astype(jnp.int32)
    ranked = jnp.cumsum(member, axis=1, dtype=jnp.int32) - 1
    slot_hit = (ranked[:, :, None] == jnp.arange(per_owner, dtype=jnp.int32)[None, None, :]).astype(
        jnp.int32
    ) * member[:, :, None]
    numbers = jnp.arange(total_strips, dtype=jnp.int32)
    return jnp.sum(slot_hit * numbers[None, :, None], axis=1, dtype=jnp.int32)


def greet(sizes):
    barrier = pltpu.get_barrier_semaphore()
    for axis, n in sizes:
        me = lax.axis_index(axis)

        def say(k, carry, axis=axis, n=n, me=me):
            pl.semaphore_signal(
                barrier, inc=1, device_id={axis: lax.rem(me + k, n)}, device_id_type=MESH
            )
            return carry

        lax.fori_loop(1, n, say, 0)
    pl.semaphore_wait(barrier, sum(n - 1 for _, n in sizes))


def all_sum(buffer, axis, n, send_sem, recv_sem):
    me = lax.axis_index(axis)

    def copy(k):
        return pltpu.make_async_remote_copy(
            src_ref=buffer.at[0],
            dst_ref=buffer.at[k],
            send_sem=send_sem.at[k],
            recv_sem=recv_sem.at[k],
            device_id={axis: lax.rem(me + k, n)},
            device_id_type=MESH,
        )

    copies = [copy(k) for k in range(1, n)]
    for c in copies:
        c.start()
    for c in copies:
        c.wait()
    total = None
    for owner in range(n):
        term = buffer[lax.rem(me - owner + n, n)]
        total = term if total is None else total + term
    return total


def swap(x):
    return pltpu.roll(x, x.shape[-1] // 2, x.ndim - 1)


def fold(x):
    return x + swap(x)


def halves(x, fields):
    return lax.broadcasted_iota(jnp.int32, x.shape, x.ndim - 1) < fields


def halo_copies(halo, rows, reach, n, send_sem, recv_sem, axis="sixteen"):
    me = lax.axis_index(axis)
    up, down = lax.rem(me + 1, n), lax.rem(me + n - 1, n)
    return [
        pltpu.make_async_remote_copy(
            src_ref=halo.at[pl.ds(rows, reach)],
            dst_ref=halo.at[pl.ds(0, reach)],
            send_sem=send_sem.at[0],
            recv_sem=recv_sem.at[0],
            device_id={axis: up},
            device_id_type=MESH,
        ),
        pltpu.make_async_remote_copy(
            src_ref=halo.at[pl.ds(reach, reach)],
            dst_ref=halo.at[pl.ds(reach + rows, reach)],
            send_sem=send_sem.at[1],
            recv_sem=recv_sem.at[1],
            device_id={axis: down},
            device_id_type=MESH,
        ),
    ]


def polish_kernel(
    nw, ns, fields, reach,
    obs, weight, scale, place, halo, place_halo, norm,
    row_eff, row_cnt, col_eff, col_cnt,
    row_buf0, row_buf1, col_buf0, col_buf1, norm_w, norm_s,
    sems_s, sems_r,
):
    rows, cols, lanes = obs.shape
    half = cols // 2
    place_rows = place.shape[0]
    place_reach = 2 * reach
    greet((("wide", nw), ("sixteen", ns)))
    place_halo[pl.ds(place_reach, place_rows)] = place[...]
    place_copies = halo_copies(
        place_halo, place_rows, place_reach, ns, sems_s.at[6], sems_r.at[6]
    )
    for c in place_copies:
        c.start()
    edge = HUBER_EDGE
    diagonal = lax.broadcasted_iota(jnp.int32, (cols, lanes), 0) == lax.broadcasted_iota(
        jnp.int32, (cols, lanes), 1
    )
    inv = 1.0 / scale[...]
    row_eff[...] = jnp.zeros_like(row_eff)
    col_eff[...] = jnp.zeros_like(col_eff)
    for sweep in range(SWEEPS):
        row_buf = (row_buf0, row_buf1)[min(sweep, 1)]
        col_buf = (col_buf0, col_buf1)[min(sweep, 1)]

        def clipped(r):
            value = (obs[r] - row_eff[pl.ds(r, 1)] - col_eff[...]) * inv
            return weight[r] * jnp.clip(value, -edge, edge)

        def row_step(r, carry):
            row_buf[0, pl.ds(r, 1)] = jnp.sum(clipped(r), axis=0, keepdims=True)
            if sweep == 0:
                row_buf[0, pl.ds(rows + r, 1)] = jnp.sum(weight[r], axis=0, keepdims=True)
            return carry

        lax.fori_loop(0, rows, row_step, 0)
        total = all_sum(row_buf, "wide", nw, sems_s.at[sweep], sems_r.at[sweep])
        if sweep == 0:
            row_cnt[...] = jnp.maximum(total[rows:], 1.0)
        row_eff[...] = row_eff[...] + scale[...] * total[:rows] / row_cnt[...]

        def col_step(r, carry):
            return carry + clipped(r)

        part = lax.fori_loop(0, rows, col_step, jnp.zeros((cols, lanes), jnp.float32))

        def packed(x):
            x = fold(x)
            low, high = x[:half], x[half:]
            return jnp.where(halves(low, fields), low, high)

        def unpacked(y):
            z = swap(y)
            first = halves(y, fields)
            return jnp.concatenate([jnp.where(first, y, z), jnp.where(first, z, y)], axis=0)

        col_buf[0, pl.ds(0, half)] = packed(part)
        if sweep == 0:
            col_buf[0, pl.ds(half, 8)] = jnp.zeros((8, lanes), jnp.float32)
            count = lax.fori_loop(
                0, rows, lambda r, c: c + weight[r], jnp.zeros((cols, lanes), jnp.float32)
            )
            col_buf[0, pl.ds(half, 1)] = jnp.sum(
                jnp.where(diagonal, fold(count), 0.0), axis=0, keepdims=True
            )
        total = all_sum(col_buf, "sixteen", ns, sems_s.at[2 + sweep], sems_r.at[2 + sweep])
        if sweep == 0:
            spread = jnp.where(diagonal, jnp.broadcast_to(total[half : half + 1], (cols, lanes)), 0.0)
            count = jnp.sum(spread, axis=1, keepdims=True)
            col_cnt[...] = jnp.maximum(jnp.broadcast_to(count, (cols, lanes)), 1.0)
        col_eff[...] = col_eff[...] + scale[...] * unpacked(total[:half]) / col_cnt[...]

    def rest(r, carry):
        value = weight[r] * (obs[r] - row_eff[pl.ds(r, 1)] - col_eff[...])
        halo[reach + r] = value
        return carry + jnp.sum(value * value, axis=0, keepdims=True)

    squares = lax.fori_loop(0, rows, rest, jnp.zeros((1, lanes), jnp.float32))
    copies = halo_copies(halo, rows, reach, ns, sems_s.at[7], sems_r.at[7])
    for c in copies:
        c.start()
    norm_w[0] = fold(squares)
    norm_s[0] = all_sum(norm_w, "wide", nw, sems_s.at[4], sems_r.at[4])
    norm[...] = all_sum(norm_s, "sixteen", ns, sems_s.at[5], sems_r.at[5])
    for c in copies + place_copies:
        c.wait()


def middle_kernel(ns, reach, row_map, halo_in, image, alpha, beta, halo, send_sem, recv_sem):
    greet((("sixteen", ns),))

    def direct(r, carry):
        before = halo_in[reach + r]
        halo[reach + r] = (before - alpha[...] * image[row_map[r]]) + beta[...] * before
        return carry

    lax.fori_loop(0, image.shape[0], direct, 0)
    copies = halo_copies(halo, image.shape[0], reach, ns, send_sem, recv_sem)
    for c in copies:
        c.start()
    for c in copies:
        c.wait()


def build_windows(halo, windows, starts, span, fields, strip_rows):
    blocks = windows.shape[1]
    pairs = strip_rows // 2

    def one(h, carry):
        for pair in range(pairs):
            for i, start in enumerate(starts):
                x = halo[h * pairs + pair, start : start + span, :]
                first = halves(x, fields)
                z = swap(x)
                for parity in range(2):
                    y = jnp.where(first, x, z) if parity == 0 else jnp.where(first, z, x)
                    high = y.astype(jnp.bfloat16).astype(jnp.float32)
                    both = jnp.where(first, high, y - high).astype(jnp.bfloat16)
                    at = (2 * pair + parity) * span
                    windows[i, h, at : at + span, :] = both
        return carry

    lax.fori_loop(0, blocks, one, 0)


def finish(i, acc, own_of, store, dots, fields, strip_rows):
    rows = strip_rows * GROUP
    y = fold(acc[:rows] + acc[rows:])
    at = pl.multiple_of(i * GROUP, GROUP)
    for pair in range(strip_rows // 2):
        even = y[(2 * pair) * GROUP : (2 * pair + 1) * GROUP]
        odd = y[(2 * pair + 1) * GROUP : (2 * pair + 2) * GROUP]
        own = own_of(pair, at)
        value = NUGGET_TERM * own + jnp.where(halves(even, fields), even, odd)
        store(pair, at, value)
        dots[0:1] += jnp.sum(own * value, axis=0, keepdims=True)
        dots[1:2] += jnp.sum(value * value, axis=0, keepdims=True)


def shifted(staged, received, n, send_sem, recv_sem):
    me = lax.axis_index("sixteen")
    return [pltpu.make_async_copy(staged.at[0], received.at[0], send_sem.at[0])] + [
        pltpu.make_async_remote_copy(
            src_ref=staged.at[k],
            dst_ref=received.at[k],
            send_sem=send_sem.at[k],
            recv_sem=recv_sem.at[k],
            device_id={"sixteen": lax.rem(me + k, n)},
            device_id_type=MESH,
        )
        for k in range(1, n)
    ]


def stage(staged, source, first, chosen):
    slots, pairs = staged.shape[:2]

    def one(k, carry):
        for pair in range(pairs):
            staged[k, pair] = source[first + chosen[k] * pairs + pair]
        return carry

    lax.fori_loop(0, slots, one, 0)


def keep(staged_image, local_image, slot, pairs, pair, at, value):
    if staged_image.shape[0] == BLOCKS_DEV:
        staged_image[slot, pair, pl.ds(at, GROUP), :] = value
    else:
        local_image[slot * pairs + pair, pl.ds(at, GROUP), :] = value


def slot_of(ns, g):
    return lax.rem(g + 1, BLOCKS_DEV) if ns == BLOCKS_DEV else g


def send_image(ns, g, images, staged_image, local_image, chosen):
    if ns == BLOCKS_DEV:
        for k in range(ns):

            @pl.when(g == (k - 1) % ns)
            def _(k=k):
                images[k].start()

    else:

        @pl.when(g == BLOCKS_DEV - 1)
        def _():
            stage(staged_image, local_image, 0, chosen)
            for c in images:
                c.start()


def first_image_kernel(
    nw, ns, starts, span, reach, fields, strip_rows,
    offs, step_block, chosen, halo, others, centre, norm,
    tiles, image, alpha, beta, norm_next, received, received_image,
    windows, dots, staged, staged_image, local_image, dot_w, dot_s,
    send_sem, recv_sem, send_image_sem, recv_image_sem, sems_s, sems_r,
):
    g = pl.program_id(0)
    slot = slot_of(ns, g)
    pairs = strip_rows // 2
    spread = 2.0 * strip_rows
    cutoff = 6.0 * strip_rows
    wide = strip_rows * span
    rows = strip_rows * GROUP

    @pl.when(g == 0)
    def _():
        stage(staged, halo, reach, chosen)
        greet((("wide", nw), ("sixteen", ns)))
        for c in shifted(staged, received, ns, send_sem, recv_sem):
            c.start()
        build_windows(halo, windows, starts, span, fields, strip_rows)
        dots[...] = jnp.zeros_like(dots)

    block = step_block[g]

    def one(i, carry):
        here = centre[block, i]
        row_here = jnp.broadcast_to(here[:, 0:1], (rows, wide))
        col_here = jnp.broadcast_to(here[:, 1:2], (rows, wide))
        acc = jnp.zeros((2 * rows, 2 * fields), jnp.float32)
        for n in range(NEIGHBOURS + 1):
            h = block + REACH + offs[n]
            pair = others[h, i]
            row_gap = pair[0:1] - row_here
            col_gap = pair[1:2] - col_here
            square = row_gap * row_gap + col_gap * col_gap
            distance = square * lax.rsqrt(jnp.maximum(square, 1e-30))
            fading = jnp.maximum(1.0 - distance * (1.0 / cutoff), 0.0)
            fading = fading * fading
            fading = fading * fading
            decay = jnp.exp2(distance * (-ROOT_THREE * LOG2E / spread))
            weight = SILL_TERM * (NEIGHBOURS + 1.0 if n == 0 else 1.0)
            lead = weight * (ROOT_THREE / spread) * distance + weight
            kernel = lead * decay * fading * (1.0 + distance * (4.0 / cutoff))
            high = kernel.astype(jnp.bfloat16)
            low = (kernel - high.astype(jnp.float32)).astype(jnp.bfloat16)
            both = jnp.concatenate([high, low], axis=0)
            tiles[0, i, :, n * wide : (n + 1) * wide] = both
            acc = acc + jnp.dot(both, windows[i, h], preferred_element_type=jnp.float32)

        def store(pair, at, value):
            image[pair, pl.ds(at, GROUP), :] = value
            keep(staged_image, local_image, slot, pairs, pair, at, value)

        def own_of(pair, at):
            return halo[reach + block * pairs + pair, pl.ds(at, GROUP), :]

        finish(i, acc, own_of, store, dots, fields, strip_rows)
        return carry

    lax.fori_loop(0, len(starts), one, 0)
    images = shifted(staged_image, received_image, ns, send_image_sem, recv_image_sem)
    send_image(ns, g, images, staged_image, local_image, chosen)

    @pl.when(g == pl.num_programs(0) - 1)
    def _():
        dot_w[0] = fold(dots[...])
        dot_s[0] = all_sum(dot_w, "wide", nw, sems_s.at[0], sems_r.at[0])
        total = all_sum(dot_s, "sixteen", ns, sems_s.at[1], sems_r.at[1])
        step = norm[...] / total[0:1]
        after = (norm[...] - 2.0 * step * total[0:1]) + step * step * total[1:2]
        alpha[...] = step
        beta[...] = after / norm[...]
        norm_next[...] = after
        for c in shifted(staged, received, ns, send_sem, recv_sem):
            c.wait()
        for c in images:
            c.wait()


def second_image_kernel(
    nw, ns, starts, span, reach, fields, strip_rows,
    offs, step_block, chosen, halo, norm, tiles,
    alpha, received_image,
    windows, dots, staged_image, local_image, dot_w, dot_s,
    send_image_sem, recv_image_sem, sems_s, sems_r,
):
    g = pl.program_id(0)
    last = pl.num_programs(0) - 1
    pairs = strip_rows // 2
    wide = strip_rows * span
    rows = strip_rows * GROUP
    slot = slot_of(ns, g)

    @pl.when(g == 0)
    def _():
        greet((("wide", nw), ("sixteen", ns)))
        build_windows(halo, windows, starts, span, fields, strip_rows)
        dots[...] = jnp.zeros_like(dots)

    block = step_block[g]

    def one(i, carry):
        acc = jnp.zeros((2 * rows, 2 * fields), jnp.float32)
        for n in range(NEIGHBOURS + 1):
            h = block + REACH + offs[n]
            acc = acc + jnp.dot(
                tiles[0, i, :, n * wide : (n + 1) * wide],
                windows[i, h],
                preferred_element_type=jnp.float32,
            )

        def store(pair, at, value):
            keep(staged_image, local_image, slot, pairs, pair, at, value)

        def own_of(pair, at):
            return halo[reach + block * pairs + pair, pl.ds(at, GROUP), :]

        finish(i, acc, own_of, store, dots, fields, strip_rows)
        return carry

    lax.fori_loop(0, len(starts), one, 0)
    images = shifted(staged_image, received_image, ns, send_image_sem, recv_image_sem)
    send_image(ns, g, images, staged_image, local_image, chosen)

    @pl.when(g == last)
    def _():
        dot_w[0] = fold(dots[...])
        dot_s[0] = all_sum(dot_w, "wide", nw, sems_s.at[0], sems_r.at[0])
        total = all_sum(dot_s, "sixteen", ns, sems_s.at[1], sems_r.at[1])
        alpha[...] = norm[...] / total[0:1]
        for c in images:
            c.wait()


def final_kernel(fields, strip_rows, came, start, middle, image, alpha0, alpha1, beta, out, rest):
    pairs, cols = start.shape[1:3]
    lead = alpha0[...] + alpha1[...] * beta[...]
    step = alpha1[...]
    for j in range(BLOCKS_DEV):
        k = came[j]
        for pair in range(pairs):
            first = start[k, pair]
            value = first - alpha0[...] * middle[k, pair]
            first = (lead * first + step * value).T
            second = (value - step * image[k, pair]).T
            for parity in range(2):
                at = (2 * pair + parity) * cols
                part = slice(parity * fields, (parity + 1) * fields)
                out[:, j, at : at + cols] = first[part]
                rest[:, j, at : at + cols] = second[part]


def on_device(observations, huber_scale, observed, jitter, owner_map, neighbours):
    fields, row_dev, col_dev = observations.shape
    nw, ns = lax.axis_size("wide"), lax.axis_size("sixteen")
    my_place = lax.axis_index("sixteen")
    group_place = lax.axis_index("wide")
    strip_rows = BLOCK // col_dev
    total_strips = BLOCKS_DEV * ns
    rows, lanes = row_dev // 2, 2 * fields
    pairs = strip_rows // 2
    reach = REACH * pairs
    f32 = jnp.float32
    shape = jax.ShapeDtypeStruct

    def pack(x):
        return x.reshape(fields, rows, 2, col_dev).transpose(1, 3, 2, 0).reshape(rows, col_dev, lanes)

    obs = pack(observations)
    weight = pack(jnp.broadcast_to(observed.astype(f32)[None], observations.shape))
    scale = jnp.concatenate([huber_scale, huber_scale])[None]
    row_place = (my_place * row_dev + jnp.arange(row_dev, dtype=jnp.int32)).astype(f32)
    col_place = (group_place * col_dev + jnp.arange(col_dev, dtype=jnp.int32)).astype(f32)
    place = jnp.stack(
        [row_place[:, None] + jitter[0], col_place[None, :] + jitter[1]], axis=1
    )
    most = max(nw, ns)
    halo, place_halo, norm = pl.pallas_call(
        functools.partial(polish_kernel, nw, ns, fields, reach),
        out_shape=(
            shape((rows + 2 * reach, col_dev, lanes), f32),
            shape((row_dev + 4 * reach, 2, col_dev), f32),
            shape((1, lanes), f32),
        ),
        in_specs=[VMEM] * 4,
        out_specs=(VMEM,) * 3,
        scratch_shapes=[
            pltpu.VMEM((rows, lanes), f32),
            pltpu.VMEM((rows, lanes), f32),
            pltpu.VMEM((col_dev, lanes), f32),
            pltpu.VMEM((col_dev, lanes), f32),
            pltpu.VMEM((nw, 2 * rows, lanes), f32),
            pltpu.VMEM((nw, rows, lanes), f32),
            pltpu.VMEM((ns, col_dev // 2 + 8, lanes), f32),
            pltpu.VMEM((ns, col_dev // 2, lanes), f32),
            pltpu.VMEM((nw, 1, lanes), f32),
            pltpu.VMEM((ns, 1, lanes), f32),
            pltpu.SemaphoreType.DMA((8, most)),
            pltpu.SemaphoreType.DMA((8, most)),
        ],
        compiler_params=pltpu.CompilerParams(collective_id=0, has_side_effects=True),
    )(obs, weight, scale, place)

    cut = 6 * strip_rows
    span = GROUP + 2 * cut
    starts = tuple(
        min(max(GROUP * i - cut, 0), col_dev - span) for i in range(col_dev // GROUP)
    )
    groups = len(starts)
    wide = strip_rows * span
    blocks_halo = BLOCKS_DEV + 2 * REACH
    by_block = place_halo.reshape(blocks_halo, strip_rows, 2, col_dev)
    others = jnp.stack([by_block[..., s : s + span] for s in starts], axis=1)
    others = others.transpose(0, 1, 3, 2, 4).reshape(blocks_halo, groups, 2, wide)
    centre = place.reshape(BLOCKS_DEV, strip_rows, 2, groups, GROUP)
    centre = centre.transpose(0, 3, 1, 4, 2).reshape(BLOCKS_DEV, groups, strip_rows * GROUP, 2)
    listed = (neighbours[0, 0] + total_strips // 2) % total_strips - total_strips // 2
    offs = jnp.concatenate([jnp.zeros((1,), jnp.int32), listed])

    tile_block = (1, groups, 2 * strip_rows * GROUP, (NEIGHBOURS + 1) * wide)
    tile_shape = shape((BLOCKS_DEV,) + tile_block[1:], jnp.bfloat16)
    whole_halo = pl.BlockSpec((rows + 2 * reach, col_dev, lanes), lambda g: (0, 0, 0))
    tile_spec = pl.BlockSpec(tile_block, lambda g: (g, 0, 0, 0))
    image_spec = pl.BlockSpec((pairs, col_dev, lanes), lambda g: (g, 0, 0))
    dots_spec = pl.BlockSpec((1, lanes), lambda g: (0, 0))
    image_shape = shape((rows, col_dev, lanes), f32)
    dots_shape = shape((1, lanes), f32)
    window_scratch = pltpu.VMEM((groups, blocks_halo, wide, lanes), jnp.bfloat16)
    static = (starts, span, reach, fields, strip_rows)
    group_map = owner_map[0]
    numbers = jnp.arange(BLOCKS_DEV, dtype=jnp.int32)
    table = owned_table(group_map, ns, BLOCKS_DEV)
    my_ids = lax.dynamic_index_in_dim(table, my_place, 0, keepdims=False)
    my_targets = lax.dynamic_slice_in_dim(group_map, my_place * BLOCKS_DEV, BLOCKS_DEV)
    owners = (my_place + jnp.arange(ns, dtype=jnp.int32)) % ns
    hit = my_targets[None, :] == owners[:, None]
    chosen = jnp.sum(hit * numbers[None], axis=1, dtype=jnp.int32)
    came = (my_place - my_ids // BLOCKS_DEV + ns) % ns
    if ns == BLOCKS_DEV:
        step_block = jnp.roll(chosen, -1)
        step_of = jnp.sum(
            (step_block[None, :] == numbers[:, None]) * numbers[None], axis=1, dtype=jnp.int32
        )
    else:
        step_block = step_of = numbers
    row_map = (step_of[:, None] * pairs + jnp.arange(pairs, dtype=jnp.int32)[None]).reshape(-1)
    anywhere = pl.BlockSpec(memory_space=pl.ANY)
    moved_shape = shape((ns, pairs, col_dev, lanes), f32)
    staging = pltpu.VMEM(moved_shape.shape, f32)

    sum_scratch = [
        pltpu.VMEM((2, lanes), f32),
        pltpu.VMEM((nw, 2, lanes), f32),
        pltpu.VMEM((ns, 2, lanes), f32),
    ]
    local = pltpu.VMEM((8, 128) if ns == BLOCKS_DEV else (rows, col_dev, lanes), f32)
    tiles, image, alpha0, beta, norm1, start, first_image = pl.pallas_call(
        functools.partial(first_image_kernel, nw, ns, *static),
        grid=(BLOCKS_DEV,),
        out_shape=(tile_shape, image_shape) + (dots_shape,) * 3 + (moved_shape,) * 2,
        in_specs=[
            SMEM,
            SMEM,
            SMEM,
            whole_halo,
            pl.BlockSpec((blocks_halo, groups, 2, wide), lambda g: (0, 0, 0, 0)),
            pl.BlockSpec((BLOCKS_DEV, groups, strip_rows * GROUP, 2), lambda g: (0, 0, 0, 0)),
            dots_spec,
        ],
        out_specs=(tile_spec, image_spec) + (dots_spec,) * 3 + (anywhere,) * 2,
        scratch_shapes=[window_scratch, sum_scratch[0], staging, staging, local]
        + sum_scratch[1:]
        + [pltpu.SemaphoreType.DMA((ns,))] * 4
        + [pltpu.SemaphoreType.DMA((2, most))] * 2,
        compiler_params=pltpu.CompilerParams(collective_id=3, has_side_effects=True),
    )(offs, step_block, chosen, halo, others, centre, norm)

    halo1 = pl.pallas_call(
        functools.partial(middle_kernel, ns, reach),
        out_shape=shape(halo.shape, f32),
        in_specs=[SMEM] + [VMEM] * 4,
        out_specs=VMEM,
        scratch_shapes=[pltpu.SemaphoreType.DMA((2,))] * 2,
        compiler_params=pltpu.CompilerParams(collective_id=1, has_side_effects=True),
    )(row_map, halo, image, alpha0, beta)
    alpha1, last_image = pl.pallas_call(
        functools.partial(second_image_kernel, nw, ns, *static),
        grid=(BLOCKS_DEV,),
        out_shape=(dots_shape, moved_shape),
        in_specs=[SMEM, SMEM, SMEM, whole_halo, dots_spec, tile_spec],
        out_specs=(dots_spec, anywhere),
        scratch_shapes=[window_scratch, sum_scratch[0], staging, local]
        + sum_scratch[1:]
        + [pltpu.SemaphoreType.DMA((ns,))] * 2
        + [pltpu.SemaphoreType.DMA((2, most))] * 2,
        compiler_params=pltpu.CompilerParams(collective_id=2, has_side_effects=True),
    )(offs, step_block, chosen, halo1, norm1, tiles)

    out_shape = shape((fields, BLOCKS_DEV, BLOCK), f32)
    solution_now, residual_now = pl.pallas_call(
        functools.partial(final_kernel, fields, strip_rows),
        out_shape=(out_shape, out_shape),
        in_specs=[SMEM] + [VMEM] * 6,
        out_specs=(VMEM, VMEM),
    )(came, start, first_image, last_image, alpha0, alpha1, beta)
    return solution_now[None, None], residual_now[None, None]


def solution(mesh):
    return jax.shard_map(
        on_device,
        mesh=mesh,
        in_specs=(
            P(None, "sixteen", "wide"),
            P(),
            P("sixteen", "wide"),
            P(None, "sixteen", "wide"),
            P("wide", None),
            P("wide", None, None),
        ),
        out_specs=(P("wide", "sixteen", None, None, None), P("wide", "sixteen", None, None, None)),
        check_vma=False,
    )
```

```python
import functools

import jax
import jax.numpy as jnp
from jax import lax
from jax.experimental import pallas as pl
from jax.experimental.pallas import tpu as pltpu
from jax.sharding import PartitionSpec as P

BLOCK = 512
BLOCKS_DEV = 8
REACH = 4
NEIGHBOURS = 6
SWEEPS = 2

HUBER_EDGE = 1.345
NUGGET_TERM = 1.0
SILL_TERM = 0.02
ROOT_THREE = 1.7320508075688772
LOG2E = 1.4426950408889634
GROUP = 16
MESH = pl.DeviceIdType.MESH
VMEM = pl.BlockSpec(memory_space=pltpu.VMEM)
SMEM = pl.BlockSpec(memory_space=pltpu.SMEM)


def owned_table(group_map, owners, per_owner):
    total_strips = group_map.shape[0]
    member = (group_map[None, :] == jnp.arange(owners, dtype=jnp.int32)[:, None]).astype(jnp.int32)
    ranked = jnp.cumsum(member, axis=1, dtype=jnp.int32) - 1
    slot_hit = (ranked[:, :, None] == jnp.arange(per_owner, dtype=jnp.int32)[None, None, :]).astype(
        jnp.int32
    ) * member[:, :, None]
    numbers = jnp.arange(total_strips, dtype=jnp.int32)
    return jnp.sum(slot_hit * numbers[None, :, None], axis=1, dtype=jnp.int32)


def greet(sizes):
    barrier = pltpu.get_barrier_semaphore()
    for axis, n in sizes:
        me = lax.axis_index(axis)

        def say(k, carry, axis=axis, n=n, me=me):
            pl.semaphore_signal(
                barrier, inc=1, device_id={axis: lax.rem(me + k, n)}, device_id_type=MESH
            )
            return carry

        lax.fori_loop(1, n, say, 0)
    pl.semaphore_wait(barrier, sum(n - 1 for _, n in sizes))


def all_sum(buffer, axis, n, send_sem, recv_sem):
    me = lax.axis_index(axis)

    def copy(k):
        return pltpu.make_async_remote_copy(
            src_ref=buffer.at[0],
            dst_ref=buffer.at[k],
            send_sem=send_sem.at[k],
            recv_sem=recv_sem.at[k],
            device_id={axis: lax.rem(me + k, n)},
            device_id_type=MESH,
        )

    copies = [copy(k) for k in range(1, n)]
    for c in copies:
        c.start()
    for c in copies:
        c.wait()
    total = None
    for owner in range(n):
        term = buffer[lax.rem(me - owner + n, n)]
        total = term if total is None else total + term
    return total


def swap(x):
    return pltpu.roll(x, x.shape[-1] // 2, x.ndim - 1)


def fold(x):
    return x + swap(x)


def halves(x, fields):
    return lax.broadcasted_iota(jnp.int32, x.shape, x.ndim - 1) < fields


def halo_copies(halo, rows, reach, n, send_sem, recv_sem, axis="sixteen"):
    me = lax.axis_index(axis)
    up, down = lax.rem(me + 1, n), lax.rem(me + n - 1, n)
    return [
        pltpu.make_async_remote_copy(
            src_ref=halo.at[pl.ds(rows, reach)],
            dst_ref=halo.at[pl.ds(0, reach)],
            send_sem=send_sem.at[0],
            recv_sem=recv_sem.at[0],
            device_id={axis: up},
            device_id_type=MESH,
        ),
        pltpu.make_async_remote_copy(
            src_ref=halo.at[pl.ds(reach, reach)],
            dst_ref=halo.at[pl.ds(reach + rows, reach)],
            send_sem=send_sem.at[1],
            recv_sem=recv_sem.at[1],
            device_id={axis: down},
            device_id_type=MESH,
        ),
    ]


def edge_copies(source, target, reach, n, send_sem, recv_sem):
    me = lax.axis_index("sixteen")
    rows = source.shape[0]
    return [
        pltpu.make_async_remote_copy(
            src_ref=source.at[pl.ds(first, reach)],
            dst_ref=target.at[pl.ds(side * reach, reach)],
            send_sem=send_sem.at[side],
            recv_sem=recv_sem.at[side],
            device_id={"sixteen": lax.rem(me + shift, n)},
            device_id_type=MESH,
        )
        for side, first, shift in ((0, rows - reach, 1), (1, 0, n - 1))
    ]


def polish_kernel(
    nw, ns, fields, reach,
    obs, weight, scale, place, halo, place_halo, norm,
    row_eff, row_cnt, col_eff, col_cnt, obs_edge, row_edge,
    row_buf0, row_buf1, col_buf0, col_buf1, norm_w, norm_s,
    sems_s, sems_r,
):
    rows, cols, lanes = obs.shape
    half = cols // 2
    place_rows = place.shape[0]
    place_reach = 2 * reach
    greet((("wide", nw), ("sixteen", ns)))
    place_halo[pl.ds(place_reach, place_rows)] = place[...]
    place_copies = halo_copies(
        place_halo, place_rows, place_reach, ns, sems_s.at[6], sems_r.at[6]
    )
    obs_copies = edge_copies(obs, obs_edge, reach, ns, sems_s.at[7], sems_r.at[7])
    row_copies = edge_copies(row_eff, row_edge, reach, ns, sems_s.at[8], sems_r.at[8])
    for c in place_copies + obs_copies:
        c.start()
    edge = HUBER_EDGE
    diagonal = lax.broadcasted_iota(jnp.int32, (cols, lanes), 0) == lax.broadcasted_iota(
        jnp.int32, (cols, lanes), 1
    )
    inv = 1.0 / scale[...]
    row_eff[...] = jnp.zeros_like(row_eff)
    col_eff[...] = jnp.zeros_like(col_eff)
    for sweep in range(SWEEPS):
        row_buf = (row_buf0, row_buf1)[min(sweep, 1)]
        col_buf = (col_buf0, col_buf1)[min(sweep, 1)]

        def clipped(r):
            value = (obs[r] - row_eff[pl.ds(r, 1)] - col_eff[...]) * inv
            return weight[r] * jnp.clip(value, -edge, edge)

        def row_step(r, carry):
            row_buf[0, pl.ds(r, 1)] = jnp.sum(clipped(r), axis=0, keepdims=True)
            if sweep == 0:
                row_buf[0, pl.ds(rows + r, 1)] = jnp.sum(weight[r], axis=0, keepdims=True)
            return carry

        lax.fori_loop(0, rows, row_step, 0)
        total = all_sum(row_buf, "wide", nw, sems_s.at[sweep], sems_r.at[sweep])
        if sweep == 0:
            row_cnt[...] = jnp.maximum(total[rows:], 1.0)
        row_eff[...] = row_eff[...] + scale[...] * total[:rows] / row_cnt[...]
        if sweep == SWEEPS - 1:
            for c in row_copies:
                c.start()

        def col_step(r, carry):
            return carry + clipped(r)

        part = lax.fori_loop(0, rows, col_step, jnp.zeros((cols, lanes), jnp.float32))

        def packed(x):
            x = fold(x)
            low, high = x[:half], x[half:]
            return jnp.where(halves(low, fields), low, high)

        def unpacked(y):
            z = swap(y)
            first = halves(y, fields)
            return jnp.concatenate([jnp.where(first, y, z), jnp.where(first, z, y)], axis=0)

        col_buf[0, pl.ds(0, half)] = packed(part)
        if sweep == 0:
            col_buf[0, pl.ds(half, 8)] = jnp.zeros((8, lanes), jnp.float32)
            count = lax.fori_loop(
                0, rows, lambda r, c: c + weight[r], jnp.zeros((cols, lanes), jnp.float32)
            )
            col_buf[0, pl.ds(half, 1)] = jnp.sum(
                jnp.where(diagonal, fold(count), 0.0), axis=0, keepdims=True
            )
        total = all_sum(col_buf, "sixteen", ns, sems_s.at[2 + sweep], sems_r.at[2 + sweep])
        if sweep == 0:
            spread = jnp.where(diagonal, jnp.broadcast_to(total[half : half + 1], (cols, lanes)), 0.0)
            count = jnp.sum(spread, axis=1, keepdims=True)
            col_cnt[...] = jnp.maximum(jnp.broadcast_to(count, (cols, lanes)), 1.0)
        col_eff[...] = col_eff[...] + scale[...] * unpacked(total[:half]) / col_cnt[...]

    def rest(r, carry):
        value = weight[r] * (obs[r] - row_eff[pl.ds(r, 1)] - col_eff[...])
        halo[reach + r] = value
        return carry + jnp.sum(value * value, axis=0, keepdims=True)

    squares = lax.fori_loop(0, rows, rest, jnp.zeros((1, lanes), jnp.float32))
    norm_w[0] = fold(squares)
    norm_s[0] = all_sum(norm_w, "wide", nw, sems_s.at[4], sems_r.at[4])
    norm[...] = all_sum(norm_s, "sixteen", ns, sems_s.at[5], sems_r.at[5])
    for c in place_copies + row_copies + obs_copies:
        c.wait()

    def across(row):
        spread = jnp.where(diagonal, jnp.broadcast_to(row, (cols, lanes)), 0.0)
        return jnp.broadcast_to(jnp.sum(spread, axis=1, keepdims=True), (cols, lanes))

    def beside(first):
        def one(q, carry):
            t = first + q
            even = across(place_halo[2 * t, 2:3])
            odd = across(place_halo[2 * t + 1, 2:3])
            seen = jnp.where(halves(even, fields), even, odd)
            at = q if first == 0 else reach + q
            halo[t] = seen * (obs_edge[at] - row_edge[pl.ds(at, 1)] - col_eff[...])
            return carry

        lax.fori_loop(0, reach, one, 0)

    beside(0)
    beside(reach + rows)


def middle_kernel(ns, reach, row_map, halo_in, image, alpha, beta, halo, send_sem, recv_sem):
    greet((("sixteen", ns),))

    def direct(r, carry):
        before = halo_in[reach + r]
        halo[reach + r] = (before - alpha[...] * image[row_map[r]]) + beta[...] * before
        return carry

    lax.fori_loop(0, image.shape[0], direct, 0)
    copies = halo_copies(halo, image.shape[0], reach, ns, send_sem, recv_sem)
    for c in copies:
        c.start()
    for c in copies:
        c.wait()


def build_windows(halo, windows, starts, span, fields, strip_rows):
    blocks = windows.shape[1]
    pairs = strip_rows // 2

    def one(h, carry):
        for pair in range(pairs):
            for i, start in enumerate(starts):
                x = halo[h * pairs + pair, start : start + span, :]
                first = halves(x, fields)
                z = swap(x)
                for parity in range(2):
                    y = jnp.where(first, x, z) if parity == 0 else jnp.where(first, z, x)
                    high = y.astype(jnp.bfloat16).astype(jnp.float32)
                    both = jnp.where(first, high, y - high).astype(jnp.bfloat16)
                    at = (2 * pair + parity) * span
                    windows[i, h, at : at + span, :] = both
        return carry

    lax.fori_loop(0, blocks, one, 0)


def finish(i, acc, own_of, store, dots, fields, strip_rows):
    rows = strip_rows * GROUP
    y = fold(acc[:rows] + acc[rows:])
    at = pl.multiple_of(i * GROUP, GROUP)
    for pair in range(strip_rows // 2):
        even = y[(2 * pair) * GROUP : (2 * pair + 1) * GROUP]
        odd = y[(2 * pair + 1) * GROUP : (2 * pair + 2) * GROUP]
        own = own_of(pair, at)
        value = NUGGET_TERM * own + jnp.where(halves(even, fields), even, odd)
        store(pair, at, value)
        dots[0:1] += jnp.sum(own * value, axis=0, keepdims=True)
        dots[1:2] += jnp.sum(value * value, axis=0, keepdims=True)


def shifted(staged, received, n, send_sem, recv_sem):
    me = lax.axis_index("sixteen")
    return [pltpu.make_async_copy(staged.at[0], received.at[0], send_sem.at[0])] + [
        pltpu.make_async_remote_copy(
            src_ref=staged.at[k],
            dst_ref=received.at[k],
            send_sem=send_sem.at[k],
            recv_sem=recv_sem.at[k],
            device_id={"sixteen": lax.rem(me + k, n)},
            device_id_type=MESH,
        )
        for k in range(1, n)
    ]


def stage(staged, source, first, chosen):
    slots, pairs = staged.shape[:2]

    def one(k, carry):
        for pair in range(pairs):
            staged[k, pair] = source[first + chosen[k] * pairs + pair]
        return carry

    lax.fori_loop(0, slots, one, 0)


def keep(staged_image, local_image, slot, pairs, pair, at, value):
    if staged_image.shape[0] == BLOCKS_DEV:
        staged_image[slot, pair, pl.ds(at, GROUP), :] = value
    else:
        local_image[slot * pairs + pair, pl.ds(at, GROUP), :] = value


def slot_of(ns, g):
    return lax.rem(g + 1, BLOCKS_DEV) if ns == BLOCKS_DEV else g


def send_image(ns, g, images, staged_image, local_image, chosen):
    if ns == BLOCKS_DEV:
        for k in range(ns):

            @pl.when(g == (k - 1) % ns)
            def _(k=k):
                images[k].start()

    else:

        @pl.when(g == BLOCKS_DEV - 1)
        def _():
            stage(staged_image, local_image, 0, chosen)
            for c in images:
                c.start()


def first_image_kernel(
    nw, ns, starts, span, reach, fields, strip_rows,
    offs, step_block, chosen, halo, others, centre, norm,
    tiles, image, alpha, beta, norm_next, received, received_image,
    windows, dots, staged, staged_image, local_image, dot_w, dot_s,
    send_sem, recv_sem, send_image_sem, recv_image_sem, sems_s, sems_r,
):
    g = pl.program_id(0)
    slot = slot_of(ns, g)
    pairs = strip_rows // 2
    spread = 2.0 * strip_rows
    cutoff = 6.0 * strip_rows
    wide = strip_rows * span
    rows = strip_rows * GROUP

    @pl.when(g == 0)
    def _():
        stage(staged, halo, reach, chosen)
        greet((("wide", nw), ("sixteen", ns)))
        for c in shifted(staged, received, ns, send_sem, recv_sem):
            c.start()
        build_windows(halo, windows, starts, span, fields, strip_rows)
        dots[...] = jnp.zeros_like(dots)

    block = step_block[g]

    def one(i, carry):
        here = centre[block, i]
        row_here = jnp.broadcast_to(here[:, 0:1], (rows, wide))
        col_here = jnp.broadcast_to(here[:, 1:2], (rows, wide))
        acc = jnp.zeros((2 * rows, 2 * fields), jnp.float32)
        for n in range(NEIGHBOURS + 1):
            h = block + REACH + offs[n]
            pair = others[h, i]
            row_gap = pair[0:1] - row_here
            col_gap = pair[1:2] - col_here
            square = row_gap * row_gap + col_gap * col_gap
            distance = square * lax.rsqrt(jnp.maximum(square, 1e-30))
            fading = jnp.maximum(1.0 - distance * (1.0 / cutoff), 0.0)
            fading = fading * fading
            fading = fading * fading
            decay = jnp.exp2(distance * (-ROOT_THREE * LOG2E / spread))
            weight = SILL_TERM * (NEIGHBOURS + 1.0 if n == 0 else 1.0)
            lead = weight * (ROOT_THREE / spread) * distance + weight
            kernel = lead * decay * fading * (1.0 + distance * (4.0 / cutoff))
            high = kernel.astype(jnp.bfloat16)
            low = (kernel - high.astype(jnp.float32)).astype(jnp.bfloat16)
            both = jnp.concatenate([high, low], axis=0)
            tiles[0, i, :, n * wide : (n + 1) * wide] = both
            acc = acc + jnp.dot(both, windows[i, h], preferred_element_type=jnp.float32)

        def store(pair, at, value):
            image[pair, pl.ds(at, GROUP), :] = value
            keep(staged_image, local_image, slot, pairs, pair, at, value)

        def own_of(pair, at):
            return halo[reach + block * pairs + pair, pl.ds(at, GROUP), :]

        finish(i, acc, own_of, store, dots, fields, strip_rows)
        return carry

    lax.fori_loop(0, len(starts), one, 0)
    images = shifted(staged_image, received_image, ns, send_image_sem, recv_image_sem)
    send_image(ns, g, images, staged_image, local_image, chosen)

    @pl.when(g == pl.num_programs(0) - 1)
    def _():
        dot_w[0] = fold(dots[...])
        dot_s[0] = all_sum(dot_w, "wide", nw, sems_s.at[0], sems_r.at[0])
        total = all_sum(dot_s, "sixteen", ns, sems_s.at[1], sems_r.at[1])
        step = norm[...] / total[0:1]
        after = (norm[...] - 2.0 * step * total[0:1]) + step * step * total[1:2]
        alpha[...] = step
        beta[...] = after / norm[...]
        norm_next[...] = after
        for c in shifted(staged, received, ns, send_sem, recv_sem):
            c.wait()
        for c in images:
            c.wait()


def second_image_kernel(
    nw, ns, starts, span, reach, fields, strip_rows,
    offs, step_block, chosen, halo, norm, tiles,
    alpha, received_image,
    windows, dots, staged_image, local_image, dot_w, dot_s,
    send_image_sem, recv_image_sem, sems_s, sems_r,
):
    g = pl.program_id(0)
    last = pl.num_programs(0) - 1
    pairs = strip_rows // 2
    wide = strip_rows * span
    rows = strip_rows * GROUP
    slot = slot_of(ns, g)

    @pl.when(g == 0)
    def _():
        greet((("wide", nw), ("sixteen", ns)))
        build_windows(halo, windows, starts, span, fields, strip_rows)
        dots[...] = jnp.zeros_like(dots)

    block = step_block[g]

    def one(i, carry):
        acc = jnp.zeros((2 * rows, 2 * fields), jnp.float32)
        for n in range(NEIGHBOURS + 1):
            h = block + REACH + offs[n]
            acc = acc + jnp.dot(
                tiles[0, i, :, n * wide : (n + 1) * wide],
                windows[i, h],
                preferred_element_type=jnp.float32,
            )

        def store(pair, at, value):
            keep(staged_image, local_image, slot, pairs, pair, at, value)

        def own_of(pair, at):
            return halo[reach + block * pairs + pair, pl.ds(at, GROUP), :]

        finish(i, acc, own_of, store, dots, fields, strip_rows)
        return carry

    lax.fori_loop(0, len(starts), one, 0)
    images = shifted(staged_image, received_image, ns, send_image_sem, recv_image_sem)
    send_image(ns, g, images, staged_image, local_image, chosen)

    @pl.when(g == last)
    def _():
        dot_w[0] = fold(dots[...])
        dot_s[0] = all_sum(dot_w, "wide", nw, sems_s.at[0], sems_r.at[0])
        total = all_sum(dot_s, "sixteen", ns, sems_s.at[1], sems_r.at[1])
        alpha[...] = norm[...] / total[0:1]
        for c in images:
            c.wait()


def final_kernel(fields, strip_rows, came, start, middle, image, alpha0, alpha1, beta, out, rest):
    pairs, cols = start.shape[1:3]
    lead = alpha0[...] + alpha1[...] * beta[...]
    step = alpha1[...]
    for j in range(BLOCKS_DEV):
        k = came[j]
        for pair in range(pairs):
            first = start[k, pair]
            value = first - alpha0[...] * middle[k, pair]
            first = (lead * first + step * value).T
            second = (value - step * image[k, pair]).T
            for parity in range(2):
                at = (2 * pair + parity) * cols
                part = slice(parity * fields, (parity + 1) * fields)
                out[:, j, at : at + cols] = first[part]
                rest[:, j, at : at + cols] = second[part]


def on_device(observations, huber_scale, observed, jitter, owner_map, neighbours):
    fields, row_dev, col_dev = observations.shape
    nw, ns = lax.axis_size("wide"), lax.axis_size("sixteen")
    my_place = lax.axis_index("sixteen")
    group_place = lax.axis_index("wide")
    strip_rows = BLOCK // col_dev
    total_strips = BLOCKS_DEV * ns
    rows, lanes = row_dev // 2, 2 * fields
    pairs = strip_rows // 2
    reach = REACH * pairs
    f32 = jnp.float32
    shape = jax.ShapeDtypeStruct

    def pack(x):
        return x.reshape(fields, rows, 2, col_dev).transpose(1, 3, 2, 0).reshape(rows, col_dev, lanes)

    obs = pack(observations)
    weight = pack(jnp.broadcast_to(observed.astype(f32)[None], observations.shape))
    scale = jnp.concatenate([huber_scale, huber_scale])[None]
    row_place = (my_place * row_dev + jnp.arange(row_dev, dtype=jnp.int32)).astype(f32)
    col_place = (group_place * col_dev + jnp.arange(col_dev, dtype=jnp.int32)).astype(f32)
    place = jnp.stack(
        [row_place[:, None] + jitter[0], col_place[None, :] + jitter[1], observed.astype(f32)],
        axis=1,
    )
    most = max(nw, ns)
    halo, place_halo, norm = pl.pallas_call(
        functools.partial(polish_kernel, nw, ns, fields, reach),
        out_shape=(
            shape((rows + 2 * reach, col_dev, lanes), f32),
            shape((row_dev + 4 * reach, 3, col_dev), f32),
            shape((1, lanes), f32),
        ),
        in_specs=[VMEM] * 4,
        out_specs=(VMEM,) * 3,
        scratch_shapes=[
            pltpu.VMEM((rows, lanes), f32),
            pltpu.VMEM((rows, lanes), f32),
            pltpu.VMEM((col_dev, lanes), f32),
            pltpu.VMEM((col_dev, lanes), f32),
            pltpu.VMEM((2 * reach, col_dev, lanes), f32),
            pltpu.VMEM((2 * reach, lanes), f32),
            pltpu.VMEM((nw, 2 * rows, lanes), f32),
            pltpu.VMEM((nw, rows, lanes), f32),
            pltpu.VMEM((ns, col_dev // 2 + 8, lanes), f32),
            pltpu.VMEM((ns, col_dev // 2, lanes), f32),
            pltpu.VMEM((nw, 1, lanes), f32),
            pltpu.VMEM((ns, 1, lanes), f32),
            pltpu.SemaphoreType.DMA((9, most)),
            pltpu.SemaphoreType.DMA((9, most)),
        ],
        compiler_params=pltpu.CompilerParams(collective_id=0, has_side_effects=True),
    )(obs, weight, scale, place)

    cut = 6 * strip_rows
    span = GROUP + 2 * cut
    starts = tuple(
        min(max(GROUP * i - cut, 0), col_dev - span) for i in range(col_dev // GROUP)
    )
    groups = len(starts)
    wide = strip_rows * span
    blocks_halo = BLOCKS_DEV + 2 * REACH
    by_block = place_halo[:, :2].reshape(blocks_halo, strip_rows, 2, col_dev)
    others = jnp.stack([by_block[..., s : s + span] for s in starts], axis=1)
    others = others.transpose(0, 1, 3, 2, 4).reshape(blocks_halo, groups, 2, wide)
    centre = place[:, :2].reshape(BLOCKS_DEV, strip_rows, 2, groups, GROUP)
    centre = centre.transpose(0, 3, 1, 4, 2).reshape(BLOCKS_DEV, groups, strip_rows * GROUP, 2)
    listed = (neighbours[0, 0] + total_strips // 2) % total_strips - total_strips // 2
    offs = jnp.concatenate([jnp.zeros((1,), jnp.int32), listed])

    tile_block = (1, groups, 2 * strip_rows * GROUP, (NEIGHBOURS + 1) * wide)
    tile_shape = shape((BLOCKS_DEV,) + tile_block[1:], jnp.bfloat16)
    whole_halo = pl.BlockSpec((rows + 2 * reach, col_dev, lanes), lambda g: (0, 0, 0))
    tile_spec = pl.BlockSpec(tile_block, lambda g: (g, 0, 0, 0))
    image_spec = pl.BlockSpec((pairs, col_dev, lanes), lambda g: (g, 0, 0))
    dots_spec = pl.BlockSpec((1, lanes), lambda g: (0, 0))
    image_shape = shape((rows, col_dev, lanes), f32)
    dots_shape = shape((1, lanes), f32)
    window_scratch = pltpu.VMEM((groups, blocks_halo, wide, lanes), jnp.bfloat16)
    static = (starts, span, reach, fields, strip_rows)
    group_map = owner_map[0]
    numbers = jnp.arange(BLOCKS_DEV, dtype=jnp.int32)
    table = owned_table(group_map, ns, BLOCKS_DEV)
    my_ids = lax.dynamic_index_in_dim(table, my_place, 0, keepdims=False)
    my_targets = lax.dynamic_slice_in_dim(group_map, my_place * BLOCKS_DEV, BLOCKS_DEV)
    owners = (my_place + jnp.arange(ns, dtype=jnp.int32)) % ns
    hit = my_targets[None, :] == owners[:, None]
    chosen = jnp.sum(hit * numbers[None], axis=1, dtype=jnp.int32)
    came = (my_place - my_ids // BLOCKS_DEV + ns) % ns
    if ns == BLOCKS_DEV:
        step_block = jnp.roll(chosen, -1)
        step_of = jnp.sum(
            (step_block[None, :] == numbers[:, None]) * numbers[None], axis=1, dtype=jnp.int32
        )
    else:
        step_block = step_of = numbers
    row_map = (step_of[:, None] * pairs + jnp.arange(pairs, dtype=jnp.int32)[None]).reshape(-1)
    anywhere = pl.BlockSpec(memory_space=pl.ANY)
    moved_shape = shape((ns, pairs, col_dev, lanes), f32)
    staging = pltpu.VMEM(moved_shape.shape, f32)

    sum_scratch = [
        pltpu.VMEM((2, lanes), f32),
        pltpu.VMEM((nw, 2, lanes), f32),
        pltpu.VMEM((ns, 2, lanes), f32),
    ]
    local = pltpu.VMEM((8, 128) if ns == BLOCKS_DEV else (rows, col_dev, lanes), f32)
    tiles, image, alpha0, beta, norm1, start, first_image = pl.pallas_call(
        functools.partial(first_image_kernel, nw, ns, *static),
        grid=(BLOCKS_DEV,),
        out_shape=(tile_shape, image_shape) + (dots_shape,) * 3 + (moved_shape,) * 2,
        in_specs=[
            SMEM,
            SMEM,
            SMEM,
            whole_halo,
            pl.BlockSpec((blocks_halo, groups, 2, wide), lambda g: (0, 0, 0, 0)),
            pl.BlockSpec((BLOCKS_DEV, groups, strip_rows * GROUP, 2), lambda g: (0, 0, 0, 0)),
            dots_spec,
        ],
        out_specs=(tile_spec, image_spec) + (dots_spec,) * 3 + (anywhere,) * 2,
        scratch_shapes=[window_scratch, sum_scratch[0], staging, staging, local]
        + sum_scratch[1:]
        + [pltpu.SemaphoreType.DMA((ns,))] * 4
        + [pltpu.SemaphoreType.DMA((2, most))] * 2,
        compiler_params=pltpu.CompilerParams(collective_id=3, has_side_effects=True),
    )(offs, step_block, chosen, halo, others, centre, norm)

    halo1 = pl.pallas_call(
        functools.partial(middle_kernel, ns, reach),
        out_shape=shape(halo.shape, f32),
        in_specs=[SMEM] + [VMEM] * 4,
        out_specs=VMEM,
        scratch_shapes=[pltpu.SemaphoreType.DMA((2,))] * 2,
        compiler_params=pltpu.CompilerParams(collective_id=1, has_side_effects=True),
    )(row_map, halo, image, alpha0, beta)
    alpha1, last_image = pl.pallas_call(
        functools.partial(second_image_kernel, nw, ns, *static),
        grid=(BLOCKS_DEV,),
        out_shape=(dots_shape, moved_shape),
        in_specs=[SMEM, SMEM, SMEM, whole_halo, dots_spec, tile_spec],
        out_specs=(dots_spec, anywhere),
        scratch_shapes=[window_scratch, sum_scratch[0], staging, local]
        + sum_scratch[1:]
        + [pltpu.SemaphoreType.DMA((ns,))] * 2
        + [pltpu.SemaphoreType.DMA((2, most))] * 2,
        compiler_params=pltpu.CompilerParams(collective_id=2, has_side_effects=True),
    )(offs, step_block, chosen, halo1, norm1, tiles)

    out_shape = shape((fields, BLOCKS_DEV, BLOCK), f32)
    solution_now, residual_now = pl.pallas_call(
        functools.partial(final_kernel, fields, strip_rows),
        out_shape=(out_shape, out_shape),
        in_specs=[SMEM] + [VMEM] * 6,
        out_specs=(VMEM, VMEM),
    )(came, start, first_image, last_image, alpha0, alpha1, beta)
    return solution_now[None, None], residual_now[None, None]


def solution(mesh):
    return jax.shard_map(
        on_device,
        mesh=mesh,
        in_specs=(
            P(None, "sixteen", "wide"),
            P(),
            P("sixteen", "wide"),
            P(None, "sixteen", "wide"),
            P("wide", None),
            P("wide", None, None),
        ),
        out_specs=(P("wide", "sixteen", None, None, None), P("wide", "sixteen", None, None, None)),
        check_vma=False,
    )
```

```python
import functools

import jax
import jax.numpy as jnp
from jax import lax
from jax.experimental import pallas as pl
from jax.experimental.pallas import tpu as pltpu
from jax.sharding import PartitionSpec as P

BLOCK = 512
BLOCKS_DEV = 8
REACH = 4
NEIGHBOURS = 6
SWEEPS = 2

HUBER_EDGE = 1.345
NUGGET_TERM = 1.0
SILL_TERM = 0.02
ROOT_THREE = 1.7320508075688772
LOG2E = 1.4426950408889634
GROUP = 16
MESH = pl.DeviceIdType.MESH
VMEM = pl.BlockSpec(memory_space=pltpu.VMEM)
SMEM = pl.BlockSpec(memory_space=pltpu.SMEM)


def owned_table(group_map, owners, per_owner):
    total_strips = group_map.shape[0]
    member = (group_map[None, :] == jnp.arange(owners, dtype=jnp.int32)[:, None]).astype(jnp.int32)
    ranked = jnp.cumsum(member, axis=1, dtype=jnp.int32) - 1
    slot_hit = (ranked[:, :, None] == jnp.arange(per_owner, dtype=jnp.int32)[None, None, :]).astype(
        jnp.int32
    ) * member[:, :, None]
    numbers = jnp.arange(total_strips, dtype=jnp.int32)
    return jnp.sum(slot_hit * numbers[None, :, None], axis=1, dtype=jnp.int32)


def greet(sizes):
    barrier = pltpu.get_barrier_semaphore()
    for axis, n in sizes:
        me = lax.axis_index(axis)

        def say(k, carry, axis=axis, n=n, me=me):
            pl.semaphore_signal(
                barrier, inc=1, device_id={axis: lax.rem(me + k, n)}, device_id_type=MESH
            )
            return carry

        lax.fori_loop(1, n, say, 0)
    pl.semaphore_wait(barrier, sum(n - 1 for _, n in sizes))


def all_sum(buffer, axis, n, send_sem, recv_sem):
    me = lax.axis_index(axis)

    def copy(k):
        return pltpu.make_async_remote_copy(
            src_ref=buffer.at[0],
            dst_ref=buffer.at[k],
            send_sem=send_sem.at[k],
            recv_sem=recv_sem.at[k],
            device_id={axis: lax.rem(me + k, n)},
            device_id_type=MESH,
        )

    copies = [copy(k) for k in range(1, n)]
    for c in copies:
        c.start()
    for c in copies:
        c.wait()
    total = None
    for owner in range(n):
        term = buffer[lax.rem(me - owner + n, n)]
        total = term if total is None else total + term
    return total


def swap(x):
    return pltpu.roll(x, x.shape[-1] // 2, x.ndim - 1)


def fold(x):
    return x + swap(x)


def halves(x, fields):
    return lax.broadcasted_iota(jnp.int32, x.shape, x.ndim - 1) < fields


def halo_copies(halo, rows, reach, n, send_sem, recv_sem, axis="sixteen"):
    me = lax.axis_index(axis)
    up, down = lax.rem(me + 1, n), lax.rem(me + n - 1, n)
    return [
        pltpu.make_async_remote_copy(
            src_ref=halo.at[pl.ds(rows, reach)],
            dst_ref=halo.at[pl.ds(0, reach)],
            send_sem=send_sem.at[0],
            recv_sem=recv_sem.at[0],
            device_id={axis: up},
            device_id_type=MESH,
        ),
        pltpu.make_async_remote_copy(
            src_ref=halo.at[pl.ds(reach, reach)],
            dst_ref=halo.at[pl.ds(reach + rows, reach)],
            send_sem=send_sem.at[1],
            recv_sem=recv_sem.at[1],
            device_id={axis: down},
            device_id_type=MESH,
        ),
    ]


def edge_copies(source, target, reach, n, send_sem, recv_sem):
    me = lax.axis_index("sixteen")
    rows = source.shape[0]
    return [
        pltpu.make_async_remote_copy(
            src_ref=source.at[pl.ds(first, reach)],
            dst_ref=target.at[pl.ds(side * reach, reach)],
            send_sem=send_sem.at[side],
            recv_sem=recv_sem.at[side],
            device_id={"sixteen": lax.rem(me + shift, n)},
            device_id_type=MESH,
        )
        for side, first, shift in ((0, rows - reach, 1), (1, 0, n - 1))
    ]


def polish_kernel(
    nw, ns, fields, reach,
    obs, weight, scale, place, halo, place_halo,
    row_eff, row_cnt, col_eff, col_cnt, obs_edge, row_edge,
    row_buf0, row_buf1, col_buf0, col_buf1,
    sems_s, sems_r,
):
    rows, cols, lanes = obs.shape
    half = cols // 2
    place_rows = place.shape[0]
    place_reach = 2 * reach
    greet((("wide", nw), ("sixteen", ns)))
    place_halo[pl.ds(place_reach, place_rows)] = place[...]
    place_copies = halo_copies(
        place_halo, place_rows, place_reach, ns, sems_s.at[6], sems_r.at[6]
    )
    obs_copies = edge_copies(obs, obs_edge, reach, ns, sems_s.at[7], sems_r.at[7])
    row_copies = edge_copies(row_eff, row_edge, reach, ns, sems_s.at[8], sems_r.at[8])
    for c in place_copies + obs_copies:
        c.start()
    edge = HUBER_EDGE
    diagonal = lax.broadcasted_iota(jnp.int32, (cols, lanes), 0) == lax.broadcasted_iota(
        jnp.int32, (cols, lanes), 1
    )
    inv = 1.0 / scale[...]
    row_eff[...] = jnp.zeros_like(row_eff)
    col_eff[...] = jnp.zeros_like(col_eff)
    for sweep in range(SWEEPS):
        row_buf = (row_buf0, row_buf1)[min(sweep, 1)]
        col_buf = (col_buf0, col_buf1)[min(sweep, 1)]

        def clipped(r):
            value = (obs[r] - row_eff[pl.ds(r, 1)] - col_eff[...]) * inv
            return weight[r] * jnp.clip(value, -edge, edge)

        def row_step(r, carry):
            row_buf[0, pl.ds(r, 1)] = jnp.sum(clipped(r), axis=0, keepdims=True)
            if sweep == 0:
                row_buf[0, pl.ds(rows + r, 1)] = jnp.sum(weight[r], axis=0, keepdims=True)
            return carry

        lax.fori_loop(0, rows, row_step, 0)
        total = all_sum(row_buf, "wide", nw, sems_s.at[sweep], sems_r.at[sweep])
        if sweep == 0:
            row_cnt[...] = jnp.maximum(total[rows:], 1.0)
        row_eff[...] = row_eff[...] + scale[...] * total[:rows] / row_cnt[...]
        if sweep == SWEEPS - 1:
            for c in row_copies:
                c.start()

        def col_step(r, carry):
            return carry + clipped(r)

        part = lax.fori_loop(0, rows, col_step, jnp.zeros((cols, lanes), jnp.float32))

        def packed(x):
            x = fold(x)
            low, high = x[:half], x[half:]
            return jnp.where(halves(low, fields), low, high)

        def unpacked(y):
            z = swap(y)
            first = halves(y, fields)
            return jnp.concatenate([jnp.where(first, y, z), jnp.where(first, z, y)], axis=0)

        col_buf[0, pl.ds(0, half)] = packed(part)
        if sweep == 0:
            col_buf[0, pl.ds(half, 8)] = jnp.zeros((8, lanes), jnp.float32)
            count = lax.fori_loop(
                0, rows, lambda r, c: c + weight[r], jnp.zeros((cols, lanes), jnp.float32)
            )
            col_buf[0, pl.ds(half, 1)] = jnp.sum(
                jnp.where(diagonal, fold(count), 0.0), axis=0, keepdims=True
            )
        total = all_sum(col_buf, "sixteen", ns, sems_s.at[2 + sweep], sems_r.at[2 + sweep])
        if sweep == 0:
            spread = jnp.where(diagonal, jnp.broadcast_to(total[half : half + 1], (cols, lanes)), 0.0)
            count = jnp.sum(spread, axis=1, keepdims=True)
            col_cnt[...] = jnp.maximum(jnp.broadcast_to(count, (cols, lanes)), 1.0)
        col_eff[...] = col_eff[...] + scale[...] * unpacked(total[:half]) / col_cnt[...]

    def rest(r, carry):
        value = weight[r] * (obs[r] - row_eff[pl.ds(r, 1)] - col_eff[...])
        halo[reach + r] = value
        return carry

    lax.fori_loop(0, rows, rest, 0)
    for c in place_copies + row_copies + obs_copies:
        c.wait()

    def across(row):
        spread = jnp.where(diagonal, jnp.broadcast_to(row, (cols, lanes)), 0.0)
        return jnp.broadcast_to(jnp.sum(spread, axis=1, keepdims=True), (cols, lanes))

    def beside(first):
        def one(q, carry):
            t = first + q
            even = across(place_halo[2 * t, 2:3])
            odd = across(place_halo[2 * t + 1, 2:3])
            seen = jnp.where(halves(even, fields), even, odd)
            at = q if first == 0 else reach + q
            halo[t] = seen * (obs_edge[at] - row_edge[pl.ds(at, 1)] - col_eff[...])
            return carry

        lax.fori_loop(0, reach, one, 0)

    beside(0)
    beside(reach + rows)


def middle_kernel(ns, reach, row_map, halo_in, image, alpha, beta, halo, send_sem, recv_sem):
    greet((("sixteen", ns),))

    def direct(r, carry):
        before = halo_in[reach + r]
        halo[reach + r] = (before - alpha[...] * image[row_map[r]]) + beta[...] * before
        return carry

    lax.fori_loop(0, image.shape[0], direct, 0)
    copies = halo_copies(halo, image.shape[0], reach, ns, send_sem, recv_sem)
    for c in copies:
        c.start()
    for c in copies:
        c.wait()


def build_windows(halo, windows, starts, span, fields, strip_rows):
    blocks = windows.shape[1]
    pairs = strip_rows // 2

    def one(h, carry):
        for pair in range(pairs):
            for i, start in enumerate(starts):
                x = halo[h * pairs + pair, start : start + span, :]
                first = halves(x, fields)
                z = swap(x)
                for parity in range(2):
                    y = jnp.where(first, x, z) if parity == 0 else jnp.where(first, z, x)
                    high = y.astype(jnp.bfloat16).astype(jnp.float32)
                    both = jnp.where(first, high, y - high).astype(jnp.bfloat16)
                    at = (2 * pair + parity) * span
                    windows[i, h, at : at + span, :] = both
        return carry

    lax.fori_loop(0, blocks, one, 0)


def finish(i, acc, own_of, store, dots, fields, strip_rows):
    rows = strip_rows * GROUP
    y = fold(acc[:rows] + acc[rows:])
    at = pl.multiple_of(i * GROUP, GROUP)
    for pair in range(strip_rows // 2):
        even = y[(2 * pair) * GROUP : (2 * pair + 1) * GROUP]
        odd = y[(2 * pair + 1) * GROUP : (2 * pair + 2) * GROUP]
        own = own_of(pair, at)
        value = NUGGET_TERM * own + jnp.where(halves(even, fields), even, odd)
        store(pair, at, value)
        dots[0:1] += jnp.sum(own * value, axis=0, keepdims=True)
        dots[1:2] += jnp.sum(value * value, axis=0, keepdims=True)
        dots[2:3] += jnp.sum(own * own, axis=0, keepdims=True)


def shifted(staged, received, n, send_sem, recv_sem):
    me = lax.axis_index("sixteen")
    return [pltpu.make_async_copy(staged.at[0], received.at[0], send_sem.at[0])] + [
        pltpu.make_async_remote_copy(
            src_ref=staged.at[k],
            dst_ref=received.at[k],
            send_sem=send_sem.at[k],
            recv_sem=recv_sem.at[k],
            device_id={"sixteen": lax.rem(me + k, n)},
            device_id_type=MESH,
        )
        for k in range(1, n)
    ]


def stage(staged, source, first, chosen):
    slots, pairs = staged.shape[:2]

    def one(k, carry):
        for pair in range(pairs):
            staged[k, pair] = source[first + chosen[k] * pairs + pair]
        return carry

    lax.fori_loop(0, slots, one, 0)


def keep(staged_image, local_image, slot, pairs, pair, at, value):
    if staged_image.shape[0] == BLOCKS_DEV:
        staged_image[slot, pair, pl.ds(at, GROUP), :] = value
    else:
        local_image[slot * pairs + pair, pl.ds(at, GROUP), :] = value


def slot_of(ns, g):
    return lax.rem(g + 1, BLOCKS_DEV) if ns == BLOCKS_DEV else g


def send_image(ns, g, images, staged_image, local_image, chosen):
    if ns == BLOCKS_DEV:
        for k in range(ns):

            @pl.when(g == (k - 1) % ns)
            def _(k=k):
                images[k].start()

    else:

        @pl.when(g == BLOCKS_DEV - 1)
        def _():
            stage(staged_image, local_image, 0, chosen)
            for c in images:
                c.start()


def first_image_kernel(
    nw, ns, starts, span, reach, fields, strip_rows,
    offs, step_block, chosen, halo, others, centre,
    tiles, image, alpha, beta, norm_next, received, received_image,
    windows, dots, staged, staged_image, local_image, dot_w, dot_s,
    send_sem, recv_sem, send_image_sem, recv_image_sem, sems_s, sems_r,
):
    g = pl.program_id(0)
    slot = slot_of(ns, g)
    pairs = strip_rows // 2
    spread = 2.0 * strip_rows
    cutoff = 6.0 * strip_rows
    wide = strip_rows * span
    rows = strip_rows * GROUP

    @pl.when(g == 0)
    def _():
        stage(staged, halo, reach, chosen)
        greet((("wide", nw), ("sixteen", ns)))
        for c in shifted(staged, received, ns, send_sem, recv_sem):
            c.start()
        build_windows(halo, windows, starts, span, fields, strip_rows)
        dots[...] = jnp.zeros_like(dots)

    block = step_block[g]

    def one(i, carry):
        here = centre[block, i]
        row_here = jnp.broadcast_to(here[:, 0:1], (rows, wide))
        col_here = jnp.broadcast_to(here[:, 1:2], (rows, wide))
        acc = jnp.zeros((2 * rows, 2 * fields), jnp.float32)
        for n in range(NEIGHBOURS + 1):
            h = block + REACH + offs[n]
            pair = others[h, i]
            row_gap = pair[0:1] - row_here
            col_gap = pair[1:2] - col_here
            square = row_gap * row_gap + col_gap * col_gap
            distance = square * lax.rsqrt(jnp.maximum(square, 1e-30))
            fading = jnp.maximum(1.0 - distance * (1.0 / cutoff), 0.0)
            fading = fading * fading
            fading = fading * fading
            decay = jnp.exp2(distance * (-ROOT_THREE * LOG2E / spread))
            weight = SILL_TERM * (NEIGHBOURS + 1.0 if n == 0 else 1.0)
            lead = weight * (ROOT_THREE / spread) * distance + weight
            kernel = lead * decay * fading * (1.0 + distance * (4.0 / cutoff))
            high = kernel.astype(jnp.bfloat16)
            low = (kernel - high.astype(jnp.float32)).astype(jnp.bfloat16)
            both = jnp.concatenate([high, low], axis=0)
            tiles[0, i, :, n * wide : (n + 1) * wide] = both
            acc = acc + jnp.dot(both, windows[i, h], preferred_element_type=jnp.float32)

        def store(pair, at, value):
            image[pair, pl.ds(at, GROUP), :] = value
            keep(staged_image, local_image, slot, pairs, pair, at, value)

        def own_of(pair, at):
            return halo[reach + block * pairs + pair, pl.ds(at, GROUP), :]

        finish(i, acc, own_of, store, dots, fields, strip_rows)
        return carry

    lax.fori_loop(0, len(starts), one, 0)
    images = shifted(staged_image, received_image, ns, send_image_sem, recv_image_sem)
    send_image(ns, g, images, staged_image, local_image, chosen)

    @pl.when(g == pl.num_programs(0) - 1)
    def _():
        dot_w[0] = fold(dots[...])
        dot_s[0] = all_sum(dot_w, "wide", nw, sems_s.at[0], sems_r.at[0])
        total = all_sum(dot_s, "sixteen", ns, sems_s.at[1], sems_r.at[1])
        norm = total[2:3]
        step = norm / total[0:1]
        after = (norm - 2.0 * step * total[0:1]) + step * step * total[1:2]
        alpha[...] = step
        beta[...] = after / norm
        norm_next[...] = after
        for c in shifted(staged, received, ns, send_sem, recv_sem):
            c.wait()
        for c in images:
            c.wait()


def second_image_kernel(
    nw, ns, starts, span, reach, fields, strip_rows,
    offs, step_block, chosen, halo, norm, tiles,
    alpha, received_image,
    windows, dots, staged_image, local_image, dot_w, dot_s,
    send_image_sem, recv_image_sem, sems_s, sems_r,
):
    g = pl.program_id(0)
    last = pl.num_programs(0) - 1
    pairs = strip_rows // 2
    wide = strip_rows * span
    rows = strip_rows * GROUP
    slot = slot_of(ns, g)

    @pl.when(g == 0)
    def _():
        greet((("wide", nw), ("sixteen", ns)))
        build_windows(halo, windows, starts, span, fields, strip_rows)
        dots[...] = jnp.zeros_like(dots)

    block = step_block[g]

    def one(i, carry):
        acc = jnp.zeros((2 * rows, 2 * fields), jnp.float32)
        for n in range(NEIGHBOURS + 1):
            h = block + REACH + offs[n]
            acc = acc + jnp.dot(
                tiles[0, i, :, n * wide : (n + 1) * wide],
                windows[i, h],
                preferred_element_type=jnp.float32,
            )

        def store(pair, at, value):
            keep(staged_image, local_image, slot, pairs, pair, at, value)

        def own_of(pair, at):
            return halo[reach + block * pairs + pair, pl.ds(at, GROUP), :]

        finish(i, acc, own_of, store, dots, fields, strip_rows)
        return carry

    lax.fori_loop(0, len(starts), one, 0)
    images = shifted(staged_image, received_image, ns, send_image_sem, recv_image_sem)
    send_image(ns, g, images, staged_image, local_image, chosen)

    @pl.when(g == last)
    def _():
        dot_w[0] = fold(dots[...])
        dot_s[0] = all_sum(dot_w, "wide", nw, sems_s.at[0], sems_r.at[0])
        total = all_sum(dot_s, "sixteen", ns, sems_s.at[1], sems_r.at[1])
        alpha[...] = norm[...] / total[0:1]
        for c in images:
            c.wait()


def final_kernel(fields, strip_rows, came, start, middle, image, alpha0, alpha1, beta, out, rest):
    pairs, cols = start.shape[1:3]
    lead = alpha0[...] + alpha1[...] * beta[...]
    step = alpha1[...]
    for j in range(BLOCKS_DEV):
        k = came[j]
        for pair in range(pairs):
            first = start[k, pair]
            value = first - alpha0[...] * middle[k, pair]
            first = (lead * first + step * value).T
            second = (value - step * image[k, pair]).T
            for parity in range(2):
                at = (2 * pair + parity) * cols
                part = slice(parity * fields, (parity + 1) * fields)
                out[:, j, at : at + cols] = first[part]
                rest[:, j, at : at + cols] = second[part]


def on_device(observations, huber_scale, observed, jitter, owner_map, neighbours):
    fields, row_dev, col_dev = observations.shape
    nw, ns = lax.axis_size("wide"), lax.axis_size("sixteen")
    my_place = lax.axis_index("sixteen")
    group_place = lax.axis_index("wide")
    strip_rows = BLOCK // col_dev
    total_strips = BLOCKS_DEV * ns
    rows, lanes = row_dev // 2, 2 * fields
    pairs = strip_rows // 2
    reach = REACH * pairs
    f32 = jnp.float32
    shape = jax.ShapeDtypeStruct

    def pack(x):
        return x.reshape(fields, rows, 2, col_dev).transpose(1, 3, 2, 0).reshape(rows, col_dev, lanes)

    obs = pack(observations)
    weight = pack(jnp.broadcast_to(observed.astype(f32)[None], observations.shape))
    scale = jnp.concatenate([huber_scale, huber_scale])[None]
    row_place = (my_place * row_dev + jnp.arange(row_dev, dtype=jnp.int32)).astype(f32)
    col_place = (group_place * col_dev + jnp.arange(col_dev, dtype=jnp.int32)).astype(f32)
    place = jnp.stack(
        [row_place[:, None] + jitter[0], col_place[None, :] + jitter[1], observed.astype(f32)],
        axis=1,
    )
    most = max(nw, ns)
    halo, place_halo = pl.pallas_call(
        functools.partial(polish_kernel, nw, ns, fields, reach),
        out_shape=(
            shape((rows + 2 * reach, col_dev, lanes), f32),
            shape((row_dev + 4 * reach, 3, col_dev), f32),
        ),
        in_specs=[VMEM] * 4,
        out_specs=(VMEM,) * 2,
        scratch_shapes=[
            pltpu.VMEM((rows, lanes), f32),
            pltpu.VMEM((rows, lanes), f32),
            pltpu.VMEM((col_dev, lanes), f32),
            pltpu.VMEM((col_dev, lanes), f32),
            pltpu.VMEM((2 * reach, col_dev, lanes), f32),
            pltpu.VMEM((2 * reach, lanes), f32),
            pltpu.VMEM((nw, 2 * rows, lanes), f32),
            pltpu.VMEM((nw, rows, lanes), f32),
            pltpu.VMEM((ns, col_dev // 2 + 8, lanes), f32),
            pltpu.VMEM((ns, col_dev // 2, lanes), f32),
            pltpu.SemaphoreType.DMA((9, most)),
            pltpu.SemaphoreType.DMA((9, most)),
        ],
        compiler_params=pltpu.CompilerParams(collective_id=0, has_side_effects=True),
    )(obs, weight, scale, place)

    cut = 6 * strip_rows
    span = GROUP + 2 * cut
    starts = tuple(
        min(max(GROUP * i - cut, 0), col_dev - span) for i in range(col_dev // GROUP)
    )
    groups = len(starts)
    wide = strip_rows * span
    blocks_halo = BLOCKS_DEV + 2 * REACH
    by_block = place_halo[:, :2].reshape(blocks_halo, strip_rows, 2, col_dev)
    others = jnp.stack([by_block[..., s : s + span] for s in starts], axis=1)
    others = others.transpose(0, 1, 3, 2, 4).reshape(blocks_halo, groups, 2, wide)
    centre = place[:, :2].reshape(BLOCKS_DEV, strip_rows, 2, groups, GROUP)
    centre = centre.transpose(0, 3, 1, 4, 2).reshape(BLOCKS_DEV, groups, strip_rows * GROUP, 2)
    listed = (neighbours[0, 0] + total_strips // 2) % total_strips - total_strips // 2
    offs = jnp.concatenate([jnp.zeros((1,), jnp.int32), listed])

    tile_block = (1, groups, 2 * strip_rows * GROUP, (NEIGHBOURS + 1) * wide)
    tile_shape = shape((BLOCKS_DEV,) + tile_block[1:], jnp.bfloat16)
    whole_halo = pl.BlockSpec((rows + 2 * reach, col_dev, lanes), lambda g: (0, 0, 0))
    tile_spec = pl.BlockSpec(tile_block, lambda g: (g, 0, 0, 0))
    image_spec = pl.BlockSpec((pairs, col_dev, lanes), lambda g: (g, 0, 0))
    dots_spec = pl.BlockSpec((1, lanes), lambda g: (0, 0))
    image_shape = shape((rows, col_dev, lanes), f32)
    dots_shape = shape((1, lanes), f32)
    window_scratch = pltpu.VMEM((groups, blocks_halo, wide, lanes), jnp.bfloat16)
    static = (starts, span, reach, fields, strip_rows)
    group_map = owner_map[0]
    numbers = jnp.arange(BLOCKS_DEV, dtype=jnp.int32)
    table = owned_table(group_map, ns, BLOCKS_DEV)
    my_ids = lax.dynamic_index_in_dim(table, my_place, 0, keepdims=False)
    my_targets = lax.dynamic_slice_in_dim(group_map, my_place * BLOCKS_DEV, BLOCKS_DEV)
    owners = (my_place + jnp.arange(ns, dtype=jnp.int32)) % ns
    hit = my_targets[None, :] == owners[:, None]
    chosen = jnp.sum(hit * numbers[None], axis=1, dtype=jnp.int32)
    came = (my_place - my_ids // BLOCKS_DEV + ns) % ns
    if ns == BLOCKS_DEV:
        step_block = jnp.roll(chosen, -1)
        step_of = jnp.sum(
            (step_block[None, :] == numbers[:, None]) * numbers[None], axis=1, dtype=jnp.int32
        )
    else:
        step_block = step_of = numbers
    row_map = (step_of[:, None] * pairs + jnp.arange(pairs, dtype=jnp.int32)[None]).reshape(-1)
    anywhere = pl.BlockSpec(memory_space=pl.ANY)
    moved_shape = shape((ns, pairs, col_dev, lanes), f32)
    staging = pltpu.VMEM(moved_shape.shape, f32)

    sum_scratch = [
        pltpu.VMEM((3, lanes), f32),
        pltpu.VMEM((nw, 3, lanes), f32),
        pltpu.VMEM((ns, 3, lanes), f32),
    ]
    local = pltpu.VMEM((8, 128) if ns == BLOCKS_DEV else (rows, col_dev, lanes), f32)
    tiles, image, alpha0, beta, norm1, start, first_image = pl.pallas_call(
        functools.partial(first_image_kernel, nw, ns, *static),
        grid=(BLOCKS_DEV,),
        out_shape=(tile_shape, image_shape) + (dots_shape,) * 3 + (moved_shape,) * 2,
        in_specs=[
            SMEM,
            SMEM,
            SMEM,
            whole_halo,
            pl.BlockSpec((blocks_halo, groups, 2, wide), lambda g: (0, 0, 0, 0)),
            pl.BlockSpec((BLOCKS_DEV, groups, strip_rows * GROUP, 2), lambda g: (0, 0, 0, 0)),
        ],
        out_specs=(tile_spec, image_spec) + (dots_spec,) * 3 + (anywhere,) * 2,
        scratch_shapes=[window_scratch, sum_scratch[0], staging, staging, local]
        + sum_scratch[1:]
        + [pltpu.SemaphoreType.DMA((ns,))] * 4
        + [pltpu.SemaphoreType.DMA((2, most))] * 2,
        compiler_params=pltpu.CompilerParams(collective_id=3, has_side_effects=True),
    )(offs, step_block, chosen, halo, others, centre)

    halo1 = pl.pallas_call(
        functools.partial(middle_kernel, ns, reach),
        out_shape=shape(halo.shape, f32),
        in_specs=[SMEM] + [VMEM] * 4,
        out_specs=VMEM,
        scratch_shapes=[pltpu.SemaphoreType.DMA((2,))] * 2,
        compiler_params=pltpu.CompilerParams(collective_id=1, has_side_effects=True),
    )(row_map, halo, image, alpha0, beta)
    alpha1, last_image = pl.pallas_call(
        functools.partial(second_image_kernel, nw, ns, *static),
        grid=(BLOCKS_DEV,),
        out_shape=(dots_shape, moved_shape),
        in_specs=[SMEM, SMEM, SMEM, whole_halo, dots_spec, tile_spec],
        out_specs=(dots_spec, anywhere),
        scratch_shapes=[window_scratch, sum_scratch[0], staging, local]
        + sum_scratch[1:]
        + [pltpu.SemaphoreType.DMA((ns,))] * 2
        + [pltpu.SemaphoreType.DMA((2, most))] * 2,
        compiler_params=pltpu.CompilerParams(collective_id=2, has_side_effects=True),
    )(offs, step_block, chosen, halo1, norm1, tiles)

    out_shape = shape((fields, BLOCKS_DEV, BLOCK), f32)
    solution_now, residual_now = pl.pallas_call(
        functools.partial(final_kernel, fields, strip_rows),
        out_shape=(out_shape, out_shape),
        in_specs=[SMEM] + [VMEM] * 6,
        out_specs=(VMEM, VMEM),
    )(came, start, first_image, last_image, alpha0, alpha1, beta)
    return solution_now[None, None], residual_now[None, None]


def solution(mesh):
    return jax.shard_map(
        on_device,
        mesh=mesh,
        in_specs=(
            P(None, "sixteen", "wide"),
            P(),
            P("sixteen", "wide"),
            P(None, "sixteen", "wide"),
            P("wide", None),
            P("wide", None, None),
        ),
        out_specs=(P("wide", "sixteen", None, None, None), P("wide", "sixteen", None, None, None)),
        check_vma=False,
    )
```
